128 devices in a mesh: group: 32 (over z, y, x_hi), head: 4 (over x_lo, core).
Axes of the slice: x: 4 (x_hi: 2, x_lo: 2; x = x_hi * 2 + x_lo), y: 4, z: 4, core: 2. Of those that a mesh axis runs over, the one named last changes fastest.
Arguments:
- tokens: bfloat16 [4, 4096, 1536], P(None, 'group'), may hold values from -6 to 6
- parents: int32 [3, 4096], P(None, 'group'), may hold values from 0 to 7
- page_request: int32 [1536], P('group'), may hold values from 0 to 511, as said below
- page_fill: int32 [1536], P('group'), may hold values from 1 to 128, as said below
- keys_pool: bfloat16 [1536, 1536, 128], P('group', 'head'), may hold values from -600 to 600
- values_pool: bfloat16 [1536, 1536, 128], P('group', 'head'), may hold values from -6 to 6
- decay_pool: bfloat16 [1536, 24, 128], P('group', 'head'), may hold values from -494.52 to 0
- gain_attn: float32 [1536], replicated, may hold values from 0.1 to 1.9
- w_query: bfloat16 [1536, 1536], P('head'), may hold values from -0.15625 to 0.15625
- w_key: bfloat16 [1536, 1536], P('head'), may hold values from -0.15625 to 0.15625
- w_value: bfloat16 [1536, 1536], P('head'), may hold values from -0.15625 to 0.15625
- w_forget: bfloat16 [1536, 24], P(None, 'head'), may hold values from -0.15625 to 0.15625
- forget_bias: float32 [24], P('head'), may hold values from -2 to 6
- w_out: bfloat16 [1536, 1536], P('head'), may hold values from -0.15625 to 0.15625
- gain_ffn: float32 [1536], replicated, may hold values from 0.1 to 1.9
- w_gate: bfloat16 [1536, 4096], P(None, 'head'), may hold values from -0.15625 to 0.15625
- w_up: bfloat16 [1536, 4096], P(None, 'head'), may hold values from -0.15625 to 0.15625
- w_down: bfloat16 [4096, 1536], P('head'), may hold values from -0.09375 to 0.09375
Outputs:
- outputs: bfloat16 [4, 4096, 1536], P(None, 'group')
The draws below stay inside these ranges and needn't reach their ends.
Inputs may be any that keep to these rules, and one draw needn't show every extreme that they name: `page_request`: request ids g * 16 to g * 16 + 15 are the requests owned by group g, and pages g * 48 to g * 48 + 47 are the page slots of group g. The first 32 slots of a group hold pages of its own requests; its other 16 slots hold pages of other groups' requests, at most 1 from the requests of one group. Every request has at least one page. `page_fill`: the valid positions of a page are its first ones.
All inputs are finite; a program needn't handle non-finite values.
Results may differ from the reference program's by a relative error of at most 0.0095.
Values may be sent and summed in bfloat16 or wider, within the bound.
A program may use at most 192 MiB of HBM per device.

```python
import math
import jax
import jax.numpy as jnp
from jax import lax

D = 1536
HEAD_TOTAL = 24
DH = 64
FF = 4096
BEAMS = 8
STEPS = 4
PAGE_POSITIONS = 128
REQ_DEV = 16
OWNED_SLOTS = 32
SPILL = 16
ROWS = 4096
PAGES_DEV = 48
PAGES = 1536
N_GROUP = 32


def layout(key):
    layout_key = jax.random.fold_in(key, 7001)
    groups = N_GROUP
    rank_group = jax.random.permutation(jax.random.fold_in(layout_key, 1), groups).astype(jnp.int32)
    rank_of = jnp.zeros((groups,), jnp.int32).at[rank_group].set(jnp.arange(groups, dtype=jnp.int32))
    long_index = jax.random.randint(jax.random.fold_in(layout_key, 2), (groups,), 0, REQ_DEV)
    long_own = jax.random.randint(jax.random.fold_in(layout_key, 3), (groups,), OWNED_SLOTS // 2, OWNED_SLOTS - REQ_DEV + 2)
    last_fills = jax.random.randint(jax.random.fold_in(layout_key, 4), (groups, REQ_DEV), 1, PAGE_POSITIONS + 1)
    last_fills = last_fills.at[rank_group[0], 0].set(1)
    page_ids = jnp.arange(groups * PAGES_DEV, dtype=jnp.int32)
    holder = page_ids // PAGES_DEV
    slot_ids = page_ids % PAGES_DEV
    first_own = long_own[holder]
    others = OWNED_SLOTS - first_own
    other_index = jnp.maximum(slot_ids - first_own, 0) * (REQ_DEV - 1) // others
    other_local = other_index + (other_index >= long_index[holder]).astype(jnp.int32)
    end_other = first_own + ((other_index + 1) * others + REQ_DEV - 2) // (REQ_DEV - 1)
    is_long = slot_ids < first_own
    own_local = jnp.where(is_long, long_index[holder], other_local)
    own_remain = jnp.where(is_long, first_own + SPILL - 1 - slot_ids, end_other - 1 - slot_ids)
    spill_slot = jnp.maximum(slot_ids - OWNED_SLOTS, 0)
    owner_rank = jnp.mod(rank_of[holder] - 1 - spill_slot % (groups - 1), groups)
    owner_group = rank_group[owner_rank]
    is_own = slot_ids < OWNED_SLOTS
    group_of = jnp.where(is_own, holder, owner_group)
    local_index = jnp.where(is_own, own_local, long_index[owner_group])
    remain = jnp.where(is_own, own_remain, SPILL - 1 - spill_slot)
    last_fill = last_fills[group_of, local_index]
    page_fills = jnp.where(remain == 0, last_fill, PAGE_POSITIONS)
    current_request = group_of * REQ_DEV + local_index
    return (current_request.astype(jnp.int32), page_fills.astype(jnp.int32), remain.astype(jnp.int32), last_fill.astype(jnp.int32))


def draw_page_request(key, part):
    current_request, page_fills, remain, last_fill = layout(key)
    return current_request


def draw_page_fill(key, part):
    current_request, page_fills, remain, last_fill = layout(key)
    return page_fills


def draw_decay_pool(key, part):
    current_request, page_fills, remain, last_fill = layout(key)
    request_total_count = N_GROUP * REQ_DEV
    log_rate = jax.random.uniform(jax.random.fold_in(key, 8101), (request_total_count, HEAD_TOTAL), minval=math.log(0.0003), maxval=math.log(0.08))
    decay_rate = jnp.exp(log_rate)[current_request]
    spike_threshold = jax.random.randint(jax.random.fold_in(key, 8104), (request_total_count, 3), 0, OWNED_SLOTS * PAGE_POSITIONS)[current_request]
    spike_discard = jax.random.uniform(jax.random.fold_in(key, 8105), (request_total_count, HEAD_TOTAL, 3), minval=0.22, maxval=0.69)[current_request]
    offset = jnp.arange(PAGE_POSITIONS, dtype=jnp.int32)
    position_gap = jnp.maximum(remain[:, None] * PAGE_POSITIONS + last_fill[:, None] - 1 - offset[None, :], 0)
    logarithm_decay = -decay_rate[:, :, None] * position_gap[:, None, :].astype(jnp.float32)
    for spike_position_index in range(3):
        spike_struck = (position_gap > spike_threshold[:, spike_position_index:spike_position_index + 1]).astype(jnp.float32)
        logarithm_decay = logarithm_decay - spike_discard[:, :, spike_position_index:spike_position_index + 1] * spike_struck[:, None, :]
    return logarithm_decay.astype(jnp.bfloat16)


def draw_keys_pool(key, part):
    page_total = N_GROUP * PAGES_DEV
    shape = (page_total, HEAD_TOTAL * DH, PAGE_POSITIONS)
    drawn_keys = jnp.clip(jax.random.normal(jax.random.fold_in(key, 8204), shape), -6.0, 6.0)
    return drawn_keys.astype(jnp.bfloat16)


def place_ends(drawn, key, low, largest):
    dims = drawn.shape
    place = [jax.random.randint(jax.random.fold_in(key, axis), (), 0, dims[axis]) for axis in range(len(dims))]
    drawn = drawn.at[tuple(place)].set(low)
    longest = dims.index(max(dims))
    place[longest] = (place[longest] + 1) % dims[longest]
    return drawn.at[tuple(place)].set(largest)


def block_levels(rng, dims, cuts, low, largest):
    level = 1.0
    for dim, blocks in cuts:
        draws = jax.random.uniform(jax.random.fold_in(jax.random.fold_in(rng, 6), dim), (blocks,), jnp.float32, low / len(cuts), largest / len(cuts))
        level = level * jnp.repeat(jnp.exp(draws), dims[dim] // blocks).reshape((-1,) + (1,) * (len(dims) - 1 - dim))
    return level


def centred(own_key, extent, width, most, pieces=(), kind=jnp.bfloat16):
    values = width * jax.random.normal(own_key, extent, jnp.float32)
    if pieces:
        values = values * block_levels(own_key, extent, pieces, -0.22, 0.18)
    return jnp.clip(values, -most, most).astype(kind)


def setup_inputs(seed: int = 0) -> dict:
    arg_keys = jax.random.split(jax.random.key(seed), 19)
    tokens = centred(arg_keys[0], (STEPS, ROWS, D), 1.0, 6.0, ((1, 32),))
    parents = place_ends(jax.random.randint(arg_keys[1], (STEPS - 1, ROWS), 0, BEAMS), jax.random.fold_in(arg_keys[1], 1), 0, BEAMS - 1).astype(jnp.int32)
    page_request = draw_page_request(jax.random.fold_in(arg_keys[18], 71), 0)
    page_fill = draw_page_fill(jax.random.fold_in(arg_keys[18], 71), 0)
    keys_pool = draw_keys_pool(jax.random.fold_in(arg_keys[18], 71), 0)
    values_pool = centred(arg_keys[5], (PAGES, HEAD_TOTAL * DH, PAGE_POSITIONS), 1.0, 6.0, ((0, 32), (1, 4)))
    decay_pool = draw_decay_pool(jax.random.fold_in(arg_keys[18], 71), 0)
    gain_attn = jnp.clip(1.0 + 0.18 * jax.random.normal(arg_keys[7], (D,), jnp.float32), 0.1, 1.9)
    w_query = centred(arg_keys[8], (HEAD_TOTAL * DH, D), D ** -0.5, 0.15625, ((0, 4),))
    w_key = centred(arg_keys[9], (HEAD_TOTAL * DH, D), D ** -0.5, 0.15625, ((0, 4),))
    w_value = centred(arg_keys[10], (HEAD_TOTAL * DH, D), D ** -0.5, 0.15625, ((0, 4),))
    w_forget = centred(arg_keys[11], (D, HEAD_TOTAL), D ** -0.5, 0.15625, ((1, 4),))
    forget_bias = jnp.clip(-2.0 + 8.0 * jax.random.uniform(arg_keys[12], (HEAD_TOTAL,), jnp.float32) ** block_levels(arg_keys[12], (HEAD_TOTAL,), ((0, 4),), -0.2, 0.2), -2.0, 6.0)
    w_out = centred(arg_keys[13], (HEAD_TOTAL * DH, D), (HEAD_TOTAL * DH) ** -0.5, 0.15625, ((0, 4),))
    gain_ffn = jnp.clip(1.0 + 0.18 * jax.random.normal(arg_keys[14], (D,), jnp.float32), 0.1, 1.9)
    w_gate = centred(arg_keys[15], (D, FF), D ** -0.5, 0.15625, ((1, 4),))
    w_up = centred(arg_keys[16], (D, FF), D ** -0.5, 0.15625, ((1, 4),))
    w_down = centred(arg_keys[17], (FF, D), FF ** -0.5, 0.09375, ((0, 4),))
    return {"tokens": tokens, "parents": parents, "page_request": page_request, "page_fill": page_fill, "keys_pool": keys_pool, "values_pool": values_pool, "decay_pool": decay_pool, "gain_attn": gain_attn, "w_query": w_query, "w_key": w_key, "w_value": w_value, "w_forget": w_forget, "forget_bias": forget_bias, "w_out": w_out, "gain_ffn": gain_ffn, "w_gate": w_gate, "w_up": w_up, "w_down": w_down}


epsilon = 1e-05
masked_score = -1e+30

def rms_scale(values, gain_vector):
    widened = values.astype(jnp.float32)
    return widened * lax.rsqrt(lax.optimization_barrier(jnp.mean(widened * widened, axis=-1, keepdims=True)) + epsilon) * gain_vector.astype(jnp.float32)

def page_block(asked_all, page_keys, page_values, page_decay, current_request, fill_count):
    page_count = page_keys.shape[0]
    asked_rows = asked_all[current_request].astype(jnp.float32)
    keys_split = page_keys.reshape(page_count, HEAD_TOTAL, DH, PAGE_POSITIONS).astype(jnp.float32)
    values_split = page_values.reshape(page_count, HEAD_TOTAL, DH, PAGE_POSITIONS).astype(jnp.float32)
    scores = jnp.einsum('psbhd,phdt->psbht', asked_rows, keys_split) * DH ** (-0.5)
    scores = scores + page_decay.astype(jnp.float32)[:, None, None, :, :]
    valid_mask = jnp.arange(PAGE_POSITIONS)[None, :] < fill_count[:, None]
    scores = jnp.where(valid_mask[:, None, None, None, :], scores, masked_score)
    page_top = lax.optimization_barrier(jnp.max(scores, axis=-1))
    weights = jnp.exp(scores - page_top[..., None])
    page_total = lax.optimization_barrier(jnp.sum(weights, axis=-1))
    rounded = lax.optimization_barrier(weights.astype(jnp.bfloat16)).astype(jnp.float32)
    numerator = jnp.einsum('psbht,phdt->psbhd', rounded, values_split)
    return (page_top, page_total, numerator)

def reference(tokens, parents, page_request, page_fill, keys_pool, values_pool, decay_pool, gain_attn, w_query, w_key, w_value, w_forget, forget_bias, w_out, gain_ffn, w_gate, w_up, w_down):
    requests = N_GROUP * REQ_DEV
    row_count = requests * BEAMS
    inner_width = HEAD_TOTAL * DH
    flat_tokens = tokens.reshape(STEPS * row_count, D)
    normed = rms_scale(flat_tokens, gain_attn).astype(jnp.bfloat16)

    def project(weight):
        return jnp.dot(normed, weight.T, preferred_element_type=jnp.float32).astype(jnp.bfloat16).reshape(STEPS, row_count, -1)
    queries = project(w_query)
    key_new = project(w_key)
    value_new = project(w_value)
    forget = jax.nn.log_sigmoid(jnp.dot(normed, w_forget, preferred_element_type=jnp.float32) + forget_bias.astype(jnp.float32)).reshape(STEPS, row_count, HEAD_TOTAL)
    asked_all = queries.reshape(STEPS, requests, BEAMS, HEAD_TOTAL, DH).transpose(1, 0, 2, 3, 4)
    blocks = (keys_pool.reshape(N_GROUP, PAGES_DEV, inner_width, PAGE_POSITIONS), values_pool.reshape(N_GROUP, PAGES_DEV, inner_width, PAGE_POSITIONS), decay_pool.reshape(N_GROUP, PAGES_DEV, HEAD_TOTAL, PAGE_POSITIONS), page_request.reshape(N_GROUP, PAGES_DEV).astype(jnp.int32), page_fill.reshape(N_GROUP, PAGES_DEV).astype(jnp.int32))

    def absorb(carry, block):
        carry_top, carry_total, carry_numer = carry
        block_keys, block_values, block_decay, block_request, block_fill = block
        page_top, page_total, numerator = page_block(asked_all, block_keys, block_values, block_decay, block_request, block_fill)
        new_top = carry_top.at[block_request].max(page_top)
        keep = jnp.exp(carry_top - new_top)
        factor = jnp.exp(page_top - new_top[block_request])
        new_total = carry_total * keep + jnp.zeros_like(carry_total).at[block_request].add(page_total * factor)
        new_numer = carry_numer * keep[..., None] + jnp.zeros_like(carry_numer).at[block_request].add(numerator * factor[..., None])
        return ((new_top, new_total, new_numer), None)
    start = (jnp.full((requests, STEPS, BEAMS, HEAD_TOTAL), masked_score, jnp.float32), jnp.zeros((requests, STEPS, BEAMS, HEAD_TOTAL), jnp.float32), jnp.zeros((requests, STEPS, BEAMS, HEAD_TOTAL, DH), jnp.float32))
    (prefix_top, prefix_total, prefix_numer), _ = lax.scan(absorb, start, blocks)
    base_rows = jnp.arange(row_count) // BEAMS * BEAMS
    hist_keys = jnp.zeros((0, row_count, inner_width), jnp.bfloat16)
    hist_values = jnp.zeros((0, row_count, inner_width), jnp.bfloat16)
    hist_totals = jnp.zeros((0, row_count, HEAD_TOTAL), jnp.float32)
    running = jnp.zeros((row_count, HEAD_TOTAL), jnp.float32)
    results = []
    for step_index in range(STEPS):
        if step_index > 0:
            source = base_rows + parents[step_index - 1]
            hist_keys = hist_keys[:, source]
            hist_values = hist_values[:, source]
            hist_totals = hist_totals[:, source]
            running = running[source]
        running = running + forget[step_index]
        hist_keys = jnp.concatenate([hist_keys, key_new[step_index][None]], axis=0)
        hist_values = jnp.concatenate([hist_values, value_new[step_index][None]], axis=0)
        hist_totals = jnp.concatenate([hist_totals, running[None]], axis=0)
        asked_now = queries[step_index].reshape(row_count, HEAD_TOTAL, DH).astype(jnp.float32)
        keys_now = hist_keys.reshape(step_index + 1, row_count, HEAD_TOTAL, DH).astype(jnp.float32)
        values_now = hist_values.reshape(step_index + 1, row_count, HEAD_TOTAL, DH).astype(jnp.float32)
        scores = jnp.einsum('rhd,urhd->rhu', asked_now, keys_now) * DH ** (-0.5) - hist_totals.transpose(1, 2, 0)
        history_top = lax.optimization_barrier(jnp.max(scores, axis=-1))
        weights = jnp.exp(scores - history_top[..., None])
        history_total = lax.optimization_barrier(jnp.sum(weights, axis=-1))
        rounded = lax.optimization_barrier(weights.astype(jnp.bfloat16)).astype(jnp.float32)
        history_numer = jnp.einsum('rhu,urhd->rhd', rounded, values_now)
        page_top = prefix_top[:, step_index].reshape(row_count, HEAD_TOTAL)
        page_total = prefix_total[:, step_index].reshape(row_count, HEAD_TOTAL)
        page_numer = prefix_numer[:, step_index].reshape(row_count, HEAD_TOTAL, DH)
        best_top = jnp.maximum(page_top, history_top)
        page_scale = jnp.exp(page_top - best_top)
        history_scale = jnp.exp(history_top - best_top)
        total_sum = page_total * page_scale + history_total * history_scale
        numer_sum = page_numer * page_scale[..., None] + history_numer * history_scale[..., None]
        attended = (numer_sum / total_sum[..., None]).astype(jnp.bfloat16).reshape(row_count, inner_width)
        residual = tokens[step_index].astype(jnp.float32) + jnp.dot(attended, w_out, preferred_element_type=jnp.float32)
        normed_ffn = rms_scale(residual, gain_ffn).astype(jnp.bfloat16)
        gate_proj = jnp.dot(normed_ffn, w_gate, preferred_element_type=jnp.float32)
        up_proj = jnp.dot(normed_ffn, w_up, preferred_element_type=jnp.float32)
        hidden = (jax.nn.silu(gate_proj) * up_proj).astype(jnp.bfloat16)
        results.append((residual + jnp.dot(hidden, w_down, preferred_element_type=jnp.float32)).astype(jnp.bfloat16))
    return jnp.stack(results, axis=0)
```

```python
import functools

import jax
import jax.numpy as jnp
from jax import lax
from jax.experimental import pallas as pl
from jax.experimental.pallas import tpu as pltpu
from jax.sharding import PartitionSpec as P

BEAMS = 8
OWNED_SLOTS = 32
SPILL = 16
STAT = 128
EPS = 1e-05
MASKED = -1e30
F32 = jnp.float32
BF16 = jnp.bfloat16
MESH = pl.DeviceIdType.MESH


def rms(x, gain):
    return x * lax.rsqrt(jnp.mean(x * x, axis=-1, keepdims=True) + EPS) * gain


def dot(a, b):
    return jnp.dot(a, b, preferred_element_type=F32)


def dot_nt(a, b):
    return lax.dot_general(a, b, (((1,), (1,)), ((), ())), preferred_element_type=F32)


def exact_dot(a, b):
    return jnp.dot(a, b, preferred_element_type=F32, precision=lax.Precision.HIGHEST)


def iota(shape, dim):
    return lax.broadcasted_iota(jnp.int32, shape, dim)


def greet(peers):
    barrier = pltpu.get_barrier_semaphore()
    count = 0
    for peer in peers:
        pl.semaphore_signal(barrier, inc=1, device_id=peer, device_id_type=MESH)
        count += 1
    pl.semaphore_wait(barrier, count)


def greet_group(groups, me):
    barrier = pltpu.get_barrier_semaphore()

    def signal(d, c):
        peer = lax.rem(me + d, groups)
        pl.semaphore_signal(barrier, inc=1, device_id={"group": peer}, device_id_type=MESH)
        return c

    lax.fori_loop(1, groups, signal, 0)
    pl.semaphore_wait(barrier, groups - 1)


def front_kernel(
    groups,
    steps,
    local,
    tokens,
    table,
    gain,
    wq,
    wk,
    wv,
    wf,
    bias,
    q_req,
    q_step,
    k_out,
    v_out,
    f_out,
    q_in,
    loc_out,
    normed,
    table_in,
    send,
    wbuf,
    wsem,
    tsend,
    trecv,
    qsend,
    qrecv,
):
    me = lax.axis_index("group")
    rows = local * BEAMS
    width = q_step.shape[-1]
    loads = [pltpu.make_async_copy(w, wbuf.at[i], wsem.at[i]) for i, w in enumerate((wq, wk, wv))]
    for load in loads:
        load.start()
    greet_group(groups, me)

    def table_copy(d, there):
        return pltpu.make_async_remote_copy(
            src_ref=table,
            dst_ref=table_in.at[there],
            send_sem=tsend.at[d],
            recv_sem=trecv.at[there],
            device_id={"group": lax.rem(me + d, groups)},
            device_id_type=MESH,
        )

    def send_table(d, c):
        table_copy(d, me).start()
        return c

    lax.fori_loop(1, groups, send_table, 0)
    table_in[pl.ds(me, 1)] = jnp.full((1,) + table_in.shape[1:], -1, jnp.int32)

    def norm_step(t, c):
        x = tokens[t].astype(F32)
        normed[t] = rms(x, gain[...]).astype(BF16)
        return c

    lax.fori_loop(0, steps, norm_step, 0)
    loads[0].wait()

    def query_step(t, c):
        q = dot_nt(normed[t], wbuf[0])
        q_step[t] = q.astype(BF16)
        return c

    lax.fori_loop(0, steps, query_step, 0)
    by_request = (
        q_step[...]
        .astype(F32)
        .reshape(steps, local, BEAMS, width)
        .transpose(1, 0, 2, 3)
        .reshape(local, steps * BEAMS, width)
    )
    q_req[...] = by_request.astype(BF16)

    def wait_table(d, c):
        table_copy(d, lax.rem(me + d, groups)).wait_recv()
        return c

    lax.fori_loop(1, groups, wait_table, 0)
    span = steps * BEAMS
    batch = 8
    flat = q_req[...].reshape(local * span, width)

    def select_batch(i, c):
        heard = table_in[pl.ds(i * batch, batch)]
        mine = heard // local == me
        where = jnp.max(jnp.where(mine, heard - me * local, -1), axis=-1, keepdims=True)
        loc_out[pl.ds(i * batch, batch)] = jnp.broadcast_to(where, (batch, 8, 128))
        tall = jnp.concatenate([where] * (span // 8), axis=1)
        shape = (batch, span, local * span)
        hit = iota(shape, 2) - iota(shape, 1) == tall * span
        pick = jnp.where(hit, 1.0, 0.0).astype(BF16).reshape(batch * span, local * span)
        send[pl.ds(i * batch, batch)] = dot(pick, flat).astype(BF16).reshape(batch, span, width)
        return c

    lax.fori_loop(0, groups // batch, select_batch, 0)

    def query_copy(d, there):
        peer = lax.rem(me + d, groups)
        return pltpu.make_async_remote_copy(
            src_ref=send.at[peer],
            dst_ref=q_in.at[there],
            send_sem=qsend.at[d],
            recv_sem=qrecv.at[there],
            device_id={"group": peer},
            device_id_type=MESH,
        )

    def send_query(d, c):
        query_copy(d, me).start()
        return c

    lax.fori_loop(1, groups, send_query, 0)
    q_in[pl.ds(me, 1)] = jnp.zeros((1,) + q_in.shape[1:], BF16)
    loads[1].wait()
    loads[2].wait()

    def rest_step(t, c):
        x = normed[t]
        k_out[t] = dot_nt(x, wbuf[1]).astype(BF16)
        v_out[t] = dot_nt(x, wbuf[2]).astype(BF16)
        gate = jax.nn.log_sigmoid(dot(x, wf[...]) + bias[...])
        heads = gate.shape[-1]
        spread = jnp.where(iota((heads, width), 1) // (width // heads) == iota((heads, width), 0), 1.0, 0.0)
        f_out[t] = exact_dot(gate, spread)
        return c

    lax.fori_loop(0, steps, rest_step, 0)

    def finish(d, c):
        table_copy(d, me).wait_send()
        query_copy(d, me).wait_send()
        query_copy(d, lax.rem(me + d, groups)).wait_recv()
        return c

    lax.fori_loop(1, groups, finish, 0)


def page_partial(q, keys, values, decay, fill, heads):
    span, width = q.shape
    low = iota((span, 128), 1) < 64
    bias = jnp.where(iota((heads, 128), 1) < fill, decay.astype(F32), MASKED)
    numer, top, total, tops, totals = [], [], [], [], []
    for j in range(width // 128):
        cut = slice(128 * j, 128 * (j + 1))
        part = q[:, cut].astype(F32) * 0.125
        wide = jnp.concatenate([jnp.where(low, part, 0.0), jnp.where(low, 0.0, part)], axis=0)
        scores = dot(wide.astype(BF16), keys[cut])
        shift = jnp.concatenate(
            [
                jnp.broadcast_to(bias[2 * j : 2 * j + 1], (span, 128)),
                jnp.broadcast_to(bias[2 * j + 1 : 2 * j + 2], (span, 128)),
            ],
            axis=0,
        )
        scores = scores + shift
        best = jnp.max(scores, axis=-1, keepdims=True)
        weight = jnp.exp(scores - best)
        whole = jnp.sum(weight, axis=-1, keepdims=True)
        out = dot_nt(weight.astype(BF16), values[cut])
        numer.append(jnp.where(low, out[:span], out[span:]))
        best = jnp.broadcast_to(best, (2 * span, 128))
        whole = jnp.broadcast_to(whole, (2 * span, 128))
        top.append(jnp.where(low, best[:span], best[span:]))
        total.append(jnp.where(low, whole[:span], whole[span:]))
        tops += [best[:span], best[span:]]
        totals += [whole[:span], whole[span:]]
    return numer, top, total, tops, totals


def pack_stats(tops, totals):
    span = tops[0].shape[0]
    lane = iota((span, STAT), 1)
    head, kind = lane % 8, lane // 8
    top = jnp.zeros((span, STAT), F32)
    total = jnp.zeros((span, STAT), F32)
    for h, (a, b) in enumerate(zip(tops, totals)):
        top = jnp.where(head == h, a, top)
        total = jnp.where(head == h, b, total)
    value = jnp.where(kind < 3, top, total)
    first = value.astype(BF16).astype(F32)
    rest = value - first
    second = rest.astype(BF16).astype(F32)
    third = rest - second
    pick = jnp.where(kind < 3, kind, kind - 3)
    out = jnp.where(pick == 0, first, jnp.where(pick == 1, second, third))
    return jnp.where(kind < 6, out, 0.0)


def attend_kernel(
    per_step, own_steps, local, heads, request, fill, q_req, q_in, keys, values, decay,
    numer_out, top_out, total_out, send_out,
):
    step = pl.program_id(0)
    width = q_req.shape[-1]
    span = q_req.shape[1]
    blocks = width // 128

    @pl.when(step == 0)
    def _():
        numer_out[...] = jnp.zeros_like(numer_out)
        top_out[...] = jnp.full_like(top_out, MASKED)
        total_out[...] = jnp.zeros_like(total_out)
        lane = iota((send_out.shape[0], span, STAT), 2)
        send_out[:, :, :width] = jnp.zeros((send_out.shape[0], span, width), BF16)
        send_out[:, :, width:] = jnp.where(lane < 8, MASKED, 0.0).astype(BF16)

    own_base = lax.axis_index("group") * local

    def own_page(i, c):
        page = step * per_step + i
        where = request[page] - own_base
        numer, top, total, _, _ = page_partial(
            q_req[where], keys.at[i], values.at[i], decay[i], fill[page], heads
        )
        for j in range(blocks):
            cut = pl.ds(128 * j, 128)
            old = top_out[where, :, cut]
            best = jnp.maximum(old, top[j])
            keep = jnp.exp(old - best)
            add = jnp.exp(top[j] - best)
            numer_out[where, :, cut] = numer_out[where, :, cut] * keep + numer[j] * add
            total_out[where, :, cut] = total_out[where, :, cut] * keep + total[j] * add
            top_out[where, :, cut] = best
        return c

    def hosted_page(i, c):
        page = step * per_step + i
        owner = request[page] // local
        numer, _, _, tops, totals = page_partial(
            q_in[owner], keys.at[i], values.at[i], decay[i], fill[page], heads
        )
        for j in range(blocks):
            send_out[owner, :, 128 * j : 128 * (j + 1)] = numer[j].astype(BF16)
        send_out[owner, :, width:] = pack_stats(tops, totals).astype(BF16)
        return c

    @pl.when(step < own_steps)
    def _():
        lax.fori_loop(0, per_step, own_page, 0)

    @pl.when(step >= own_steps)
    def _():
        lax.fori_loop(0, per_step, hosted_page, 0)


def history(q, k, v, f, parents, numer_out, top_out, total_out, heads):
    steps, rows, width = q.shape
    size = width // heads
    square = (width, width)
    same = jnp.where(iota(square, 0) // size == iota(square, 1) // size, 1.0, 0.0).astype(BF16)
    keys, vals, sums = [], [], []
    for t in range(steps):
        if t > 0:
            lane = iota((rows, rows), 1)
            source = lane - lane % BEAMS + parents[t - 1 : t]
            pick = jnp.where(iota((rows, rows), 0) == source, 1.0, 0.0).T
            pick16 = pick.astype(BF16)
            keys = [dot(pick16, a).astype(BF16) for a in keys]
            vals = [dot(pick16, a).astype(BF16) for a in vals]
            sums = [exact_dot(pick, a) for a in sums]
        keys.append(k[t])
        vals.append(v[t])
        sums.append(f[t] + sums[-1] if t > 0 else f[t])
        asked = q[t].astype(F32)
        scores = []
        for key, total in zip(keys, sums):
            product = asked * key.astype(F32)
            high = product.astype(BF16)
            low = (product - high.astype(F32)).astype(BF16)
            scores.append((dot(high, same) + dot(low, same)) * size ** (-0.5) - total)
        best = functools.reduce(jnp.maximum, scores)
        weights = [jnp.exp(s - best) for s in scores]
        top_out[t] = best
        total_out[t] = functools.reduce(jnp.add, weights)
        numer_out[t] = functools.reduce(
            jnp.add, [w.astype(BF16).astype(F32) * a.astype(F32) for w, a in zip(weights, vals)]
        )


def return_kernel(
    groups, heads, sent, q, k, v, f, parents, arrived, numer_out, top_out, total_out, ssem, rsem
):
    me = lax.axis_index("group")
    greet_group(groups, me)

    def copy(d, there):
        peer = lax.rem(me + d, groups)
        return pltpu.make_async_remote_copy(
            src_ref=sent.at[peer],
            dst_ref=arrived.at[there],
            send_sem=ssem.at[d],
            recv_sem=rsem.at[there],
            device_id={"group": peer},
            device_id_type=MESH,
        )

    def start(d, c):
        copy(d, me).start()
        return c

    lax.fori_loop(1, groups, start, 0)
    arrived[pl.ds(me, 1)] = jnp.zeros((1,) + arrived.shape[1:], BF16)
    history(q, k, v, f, parents, numer_out, top_out, total_out, heads)

    def finish(d, c):
        copy(d, me).wait_send()
        copy(d, lax.rem(me + d, groups)).wait_recv()
        return c

    lax.fori_loop(1, groups, finish, 0)


def combine_kernel(
    heads, where, arrived, numer_in, top_in, total_in, h_numer, h_top, h_total,
    out, numer, top, total, stats, final,
):
    groups, span, full = arrived.shape
    local, _, width = numer_in.shape
    steps = h_numer.shape[0]
    size = width // heads
    numer[...] = numer_in[...]
    top[...] = top_in[...]
    total[...] = total_in[...]
    shape = (STAT, 2 * width)
    lane, col = iota(shape, 0), iota(shape, 1)
    second = jnp.where(col >= width, 1, 0)
    spread = (lane // 8 // 3 == second) & (lane % 8 == (col - second * width) // size)
    spread = jnp.where(spread, 1.0, 0.0).astype(BF16)
    batch = 8

    def expand(i, c):
        block = arrived[pl.ds(i * batch, batch), :, width:].reshape(batch * span, STAT)
        stats[pl.ds(i * batch, batch)] = dot(block, spread).reshape(batch, span, 2 * width)
        return c

    lax.fori_loop(0, groups // batch, expand, 0)

    def absorb(g, c):
        r = where[g]

        @pl.when(r >= 0)
        def _():
            old = top[r]
            new = stats[g, :, :width]
            best = jnp.maximum(old, new)
            keep = jnp.exp(old - best)
            add = jnp.exp(new - best)
            numer[r] = numer[r] * keep + arrived[g, :, :width].astype(F32) * add
            total[r] = total[r] * keep + stats[g, :, width:] * add
            top[r] = best

        return c

    lax.fori_loop(0, groups, absorb, 0)

    def close(r, c):
        cut = pl.ds(pl.multiple_of(r * BEAMS, BEAMS), BEAMS)
        shape = (steps, BEAMS, width)
        p_top = top[r].reshape(shape)
        best = jnp.maximum(p_top, h_top[:, cut])
        p_scale = jnp.exp(p_top - best)
        h_scale = jnp.exp(h_top[:, cut] - best)
        whole = total[r].reshape(shape) * p_scale + h_total[:, cut] * h_scale
        mixed = numer[r].reshape(shape) * p_scale + h_numer[:, cut] * h_scale
        final[:, cut] = mixed / whole
        return c

    lax.fori_loop(0, local, close, 0)
    out[...] = final[...].astype(BF16)


def tail_kernel(
    att, tokens, gain, wo_h, wg_h, wu_h, wd_h, out,
    wo, wg, wu, wd, keep, resid, normed, acc,
    a_tx, a_rx, b_tx, b_rx, c_tx, c_rx, d_tx, d_rx,
    wsem, sems_s, sems_r,
):
    steps, rows, model = out.shape
    half = rows // 2
    me = lax.axis_index("head")
    core = lax.rem(me, 2)
    sibling = {"head": me + 1 - 2 * core}
    chip = me // 2
    across = {"head": core + 2 * (1 - chip)}
    mine = pl.ds(pl.multiple_of(core * half, half), half)
    theirs = pl.ds(pl.multiple_of((1 - core) * half, half), half)
    loads = [
        pltpu.make_async_copy(a, b, wsem.at[i])
        for i, (a, b) in enumerate(((wo_h, wo), (wg_h, wg), (wu_h, wu), (wd_h, wd)))
    ]
    for load in loads:
        load.start()
    greet((sibling, across))

    def remote(kind, t, src, dst, device):
        return pltpu.make_async_remote_copy(
            src_ref=src,
            dst_ref=dst,
            send_sem=sems_s.at[kind, t],
            recv_sem=sems_r.at[kind, t],
            device_id=device,
            device_id_type=MESH,
        )

    copy_a = lambda t: remote(0, t, a_tx.at[t], a_rx.at[t], sibling)
    copy_b = lambda t: remote(1, t, b_tx.at[t], b_rx.at[t], across)
    copy_n = lambda t: remote(2, t, normed.at[t, mine], normed.at[t, mine], sibling)
    copy_n_in = lambda t: remote(2, t, normed.at[t, theirs], normed.at[t, theirs], sibling)
    copy_c = lambda t: remote(3, t, c_tx.at[t], c_rx.at[t], sibling)
    copy_d = lambda t: remote(4, t, d_tx.at[t], d_rx.at[t], across)
    copy_o = lambda t: remote(5, t, out.at[t, mine], out.at[t, mine], sibling)
    copy_o_in = lambda t: remote(5, t, out.at[t, theirs], out.at[t, theirs], sibling)

    loads[0].wait()

    def project(t, c):
        acc[...] = dot(att[t], wo[...])
        keep[t] = acc[mine]
        a_tx[t] = acc[theirs].astype(BF16)
        copy_a(t).start()
        return c

    lax.fori_loop(0, steps, project, 0)

    def cross(t, c):
        copy_a(t).wait_recv()
        b_tx[t] = (keep[t] + a_rx[t].astype(F32)).astype(BF16)
        copy_b(t).start()
        return c

    lax.fori_loop(0, steps, cross, 0)
    for load in loads[1:]:
        load.wait()

    def down_cross(t):
        copy_c(t).wait_recv()
        d_tx[t] = (keep[t] + c_rx[t].astype(F32)).astype(BF16)
        copy_d(t).start()

    def feed(t, c):
        copy_b(t).wait_recv()
        res = tokens[t, mine].astype(F32) + (b_tx[t].astype(F32) + b_rx[t].astype(F32))
        resid[t] = res
        normed[t, mine] = rms(res, gain[...]).astype(BF16)
        copy_n(t).start()

        @pl.when(t > 0)
        def _():
            down_cross(t - 1)

        copy_n_in(t).wait_recv()
        x = normed[t]
        gate = dot(x, wg[...])
        up = dot(x, wu[...])
        hidden = (gate / (1.0 + jnp.exp(-gate)) * up).astype(BF16)
        acc[...] = dot(hidden, wd[...])
        keep[t] = acc[mine]
        c_tx[t] = acc[theirs].astype(BF16)
        copy_c(t).start()
        return c

    lax.fori_loop(0, steps, feed, 0)
    down_cross(steps - 1)

    def close(t, c):
        copy_d(t).wait_recv()
        total = resid[t] + (d_tx[t].astype(F32) + d_rx[t].astype(F32))
        out[t, mine] = total.astype(BF16)
        copy_o(t).start()
        return c

    lax.fori_loop(0, steps, close, 0)

    def finish(t, c):
        copy_o_in(t).wait_recv()
        copy_a(t).wait_send()
        copy_b(t).wait_send()
        copy_n(t).wait_send()
        copy_c(t).wait_send()
        copy_d(t).wait_send()
        copy_o(t).wait_send()
        return c

    lax.fori_loop(0, steps, finish, 0)


VM = pl.BlockSpec(memory_space=pltpu.VMEM)
SM = pl.BlockSpec(memory_space=pltpu.SMEM)
HB = pl.BlockSpec(memory_space=pl.ANY)
DMA = pltpu.SemaphoreType.DMA
LIMIT = 56 << 20


def params(**kw):
    return pltpu.CompilerParams(vmem_limit_bytes=LIMIT, **kw)


def shards(
    tokens, parents, page_request, page_fill, keys_pool, values_pool, decay_pool, gain_attn,
    w_query, w_key, w_value, w_forget, forget_bias, w_out, gain_ffn, w_gate, w_up, w_down,
):
    steps, rows, model = tokens.shape
    heads = w_forget.shape[1]
    width = w_query.shape[0]
    local = rows // BEAMS
    span = steps * BEAMS
    groups = lax.axis_size("group")
    pages = page_request.shape[0]
    ff = w_gate.shape[1]
    sds = jax.ShapeDtypeStruct

    hosted = jnp.full((8, 128), -1, jnp.int32).at[:, :SPILL].set(page_request[OWNED_SLOTS:][None])
    q_req, q_step, k_new, v_new, f_new, q_in, loc = pl.pallas_call(
        functools.partial(front_kernel, groups, steps, local),
        out_shape=(
            sds((local, span, width), BF16),
            sds((steps, rows, width), BF16),
            sds((steps, rows, width), BF16),
            sds((steps, rows, width), BF16),
            sds((steps, rows, width), F32),
            sds((groups, span, width), BF16),
            sds((groups, 8, 128), jnp.int32),
        ),
        in_specs=[VM, VM, VM, HB, HB, HB, VM, VM],
        out_specs=(VM,) * 7,
        scratch_shapes=[
            pltpu.VMEM((steps, rows, model), BF16),
            pltpu.VMEM((groups, 8, 128), jnp.int32),
            pltpu.VMEM((groups, span, width), BF16),
            pltpu.VMEM((3, width, model), BF16),
            DMA((3,)),
            DMA((groups,)),
            DMA((groups,)),
            DMA((groups,)),
            DMA((groups,)),
        ],
        compiler_params=params(collective_id=0, has_side_effects=True),
        name="front",
    )(tokens, hosted, gain_attn[None], w_query, w_key, w_value, w_forget, forget_bias[None])

    per_step = 8
    whole = lambda shape: pl.BlockSpec(shape, lambda i, *_: (0,) * len(shape))
    paged = lambda shape: pl.BlockSpec((per_step,) + shape, lambda i, *_: (i, 0, 0))
    state = (local, span, width)
    p_numer, p_top, p_total, sent = pl.pallas_call(
        functools.partial(attend_kernel, per_step, OWNED_SLOTS // per_step, local, heads),
        out_shape=(sds(state, F32),) * 3 + (sds((groups, span, width + STAT), BF16),),
        grid_spec=pltpu.PrefetchScalarGridSpec(
            num_scalar_prefetch=2,
            grid=(pages // per_step,),
            in_specs=[
                whole(state),
                whole((groups, span, width)),
                paged(keys_pool.shape[1:]),
                paged(values_pool.shape[1:]),
                paged(decay_pool.shape[1:]),
            ],
            out_specs=(whole(state),) * 3 + (whole((groups, span, width + STAT)),),
        ),
        compiler_params=params(),
        name="attend",
    )(page_request, page_fill, q_req, q_in, keys_pool, values_pool, decay_pool)

    arrived, h_numer, h_top, h_total = pl.pallas_call(
        functools.partial(return_kernel, groups, heads),
        out_shape=(sds((groups, span, width + STAT), BF16),) + (sds((steps, rows, width), F32),) * 3,
        in_specs=[VM] * 6,
        out_specs=(VM,) * 4,
        scratch_shapes=[DMA((groups,)), DMA((groups,))],
        compiler_params=params(collective_id=1, has_side_effects=True),
        name="bring",
    )(sent, q_step, k_new, v_new, f_new, parents)

    attended = pl.pallas_call(
        functools.partial(combine_kernel, heads),
        out_shape=sds((steps, rows, width), BF16),
        in_specs=[SM] + [VM] * 7,
        out_specs=VM,
        scratch_shapes=[pltpu.VMEM(state, F32)] * 3
        + [pltpu.VMEM((groups, span, 2 * width), F32), pltpu.VMEM((steps, rows, width), F32)],
        compiler_params=params(),
        name="combine",
    )(loc[:, 0, 0], arrived, p_numer, p_top, p_total, h_numer, h_top, h_total)

    half = (steps, rows // 2, model)
    return pl.pallas_call(
        tail_kernel,
        out_shape=sds((steps, rows, model), BF16),
        in_specs=[VM, VM, VM, HB, HB, HB, HB],
        out_specs=VM,
        scratch_shapes=[
            pltpu.VMEM((width, model), BF16),
            pltpu.VMEM((model, ff), BF16),
            pltpu.VMEM((model, ff), BF16),
            pltpu.VMEM((ff, model), BF16),
            pltpu.VMEM(half, F32),
            pltpu.VMEM(half, F32),
            pltpu.VMEM((steps, rows, model), BF16),
            pltpu.VMEM((rows, model), F32),
        ]
        + [pltpu.VMEM(half, BF16)] * 8
        + [DMA((4,)), DMA((6, steps)), DMA((6, steps))],
        compiler_params=params(collective_id=2, has_side_effects=True),
        name="tail",
    )(attended, tokens, gain_ffn[None], w_out, w_gate, w_up, w_down)


def solution(mesh):
    return jax.shard_map(
        shards,
        mesh=mesh,
        in_specs=(
            P(None, "group", None),
            P(None, "group"),
            P("group"),
            P("group"),
            P("group", "head", None),
            P("group", "head", None),
            P("group", "head", None),
            P(),
            P("head", None),
            P("head", None),
            P("head", None),
            P(None, "head"),
            P("head"),
            P("head", None),
            P(),
            P(None, "head"),
            P(None, "head"),
            P("head", None),
        ),
        out_specs=P(None, "group", None),
        check_vma=False,
    )
```

```python
import functools

import jax
import jax.numpy as jnp
from jax import lax
from jax.experimental import pallas as pl
from jax.experimental.pallas import tpu as pltpu
from jax.sharding import PartitionSpec as P

BEAMS = 8
OWNED_SLOTS = 32
SPILL = 16
STAT = 128
EPS = 1e-05
MASKED = -1e30
F32 = jnp.float32
BF16 = jnp.bfloat16
MESH = pl.DeviceIdType.MESH


def rms(x, gain):
    return x * lax.rsqrt(jnp.mean(x * x, axis=-1, keepdims=True) + EPS) * gain


def dot(a, b):
    return jnp.dot(a, b, preferred_element_type=F32)


def dot_nt(a, b):
    return lax.dot_general(a, b, (((1,), (1,)), ((), ())), preferred_element_type=F32)


def exact_dot(a, b):
    return jnp.dot(a, b, preferred_element_type=F32, precision=lax.Precision.HIGHEST)


def iota(shape, dim):
    return lax.broadcasted_iota(jnp.int32, shape, dim)


def greet(peers):
    barrier = pltpu.get_barrier_semaphore()
    count = 0
    for peer in peers:
        pl.semaphore_signal(barrier, inc=1, device_id=peer, device_id_type=MESH)
        count += 1
    pl.semaphore_wait(barrier, count)


def greet_group(groups, me):
    barrier = pltpu.get_barrier_semaphore()

    def signal(d, c):
        peer = lax.rem(me + d, groups)
        pl.semaphore_signal(barrier, inc=1, device_id={"group": peer}, device_id_type=MESH)
        return c

    lax.fori_loop(1, groups, signal, 0)
    pl.semaphore_wait(barrier, groups - 1)


def page_partial(q, masks, keys, values, bias):
    span, width = q.shape
    low = iota((span, 128), 1) < 64
    numer, top, total, tops, totals = [], [], [], [], []
    for j in range(width // 128):
        cut = slice(128 * j, 128 * (j + 1))
        wide = jnp.concatenate([q[:, cut]] * 2, axis=0) * masks
        shift = jnp.concatenate([jnp.broadcast_to(b, (span, 128)) for b in bias[2 * j : 2 * j + 2]], axis=0)
        scores = dot(wide, keys[cut]) + shift
        best = jnp.max(scores, axis=-1, keepdims=True)
        weight = jnp.exp(scores - best)
        whole = jnp.sum(weight, axis=-1, keepdims=True)
        out = dot(weight.astype(BF16), values[cut].astype(F32).T.astype(BF16))
        numer.append(jnp.where(low, out[:span], out[span:]))
        best = jnp.broadcast_to(best, (2 * span, 128))
        whole = jnp.broadcast_to(whole, (2 * span, 128))
        top.append(jnp.where(low, best[:span], best[span:]))
        total.append(jnp.where(low, whole[:span], whole[span:]))
        tops += [best[:span], best[span:]]
        totals += [whole[:span], whole[span:]]
    return numer, top, total, tops, totals


def pack_stats(tops, totals):
    span = tops[0].shape[0]
    lane = iota((span, STAT), 1)
    head, kind = lane % 8, lane // 8
    value = jnp.zeros((span, STAT), F32)
    for h, (a, b) in enumerate(zip(tops, totals)):
        value = jnp.where(head == h, jnp.where(kind < 3, a, b), value)
    first = value.astype(BF16).astype(F32)
    rest = value - first
    second = rest.astype(BF16).astype(F32)
    third = rest - second
    pick = jnp.where(kind < 3, kind, kind - 3)
    out = jnp.where(pick == 0, first, jnp.where(pick == 1, second, third))
    return jnp.where(kind < 6, out, 0.0)


def history(q, k, v, f, parents, numer_out, top_out, total_out, heads):
    steps, rows, width = q.shape
    size = width // heads
    square = (width, width)
    same = jnp.where(iota(square, 0) // size == iota(square, 1) // size, 1.0, 0.0).astype(BF16)
    keys, vals, sums = [], [], []
    for t in range(steps):
        if t > 0:
            lane = iota((rows, rows), 1)
            source = lane - lane % BEAMS + parents[t - 1 : t]
            pick = jnp.where(iota((rows, rows), 0) == source, 1.0, 0.0).T
            pick16 = pick.astype(BF16)
            keys = [dot(pick16, a).astype(BF16) for a in keys]
            vals = [dot(pick16, a).astype(BF16) for a in vals]
            sums = [exact_dot(pick, a) for a in sums]
        keys.append(k[t])
        vals.append(v[t])
        sums.append(f[t] + sums[-1] if t > 0 else f[t])
        asked = q[t].astype(F32)
        scores = []
        for key, total in zip(keys, sums):
            product = asked * key.astype(F32)
            high = product.astype(BF16)
            low = (product - high.astype(F32)).astype(BF16)
            scores.append((dot(high, same) + dot(low, same)) - total)
        best = functools.reduce(jnp.maximum, scores)
        weights = [jnp.exp(s - best) for s in scores]
        top_out[t] = best
        total_out[t] = functools.reduce(jnp.add, weights)
        numer_out[t] = functools.reduce(
            jnp.add, [w.astype(BF16).astype(F32) * a.astype(F32) for w, a in zip(weights, vals)]
        )


def group_kernel(
    groups, local, heads, request, fill, tokens_h, gain, wq, wk, wv, wf, bias, parents, keys_h, values_h, decay,
    att,
    tokens, wbuf, keys, values, dec, normed, q_req, q_step, k_new, v_new, f_new,
    table, table_in, loc_v, send, q_in, sent, arrived, s_numer, s_top, s_total, h_numer, h_top, h_total, final,
    loc, last, slot,
    lsem, msem, tsend, trecv, qsend, qrecv, rsend, rrecv,
):
    steps, rows, width = q_step.shape
    span = steps * BEAMS
    pages = keys.shape[0]
    owned = pages - SPILL
    size = width // heads
    blocks = width // 128
    me = lax.axis_index("group")
    loads = [
        pltpu.make_async_copy(a, b, lsem.at[i])
        for i, (a, b) in enumerate(
            (
                (tokens_h, tokens),
                (wq, wbuf.at[0]),
                (wk, wbuf.at[1]),
                (wv, wbuf.at[2]),
                (keys_h, keys),
                (values_h, values),
            )
        )
    ]
    for load in loads:
        load.start()
    barrier = pltpu.get_barrier_semaphore()

    def peer_of(d):
        return lax.rem(me + d, groups)

    def each_peer(body):
        def step(d, c):
            body(d)
            return c

        lax.fori_loop(1, groups, step, 0)

    each_peer(
        lambda d: pl.semaphore_signal(
            barrier, inc=1, device_id={"group": peer_of(d)}, device_id_type=MESH
        )
    )

    def remote(src, dst, ssem, rsem, d):
        return pltpu.make_async_remote_copy(
            src_ref=src,
            dst_ref=dst,
            send_sem=ssem,
            recv_sem=rsem,
            device_id={"group": peer_of(d)},
            device_id_type=MESH,
        )

    def table_copy(d, there):
        return remote(table, table_in.at[there], tsend.at[d], trecv.at[there], d)

    def query_copy(d, there):
        return remote(send.at[peer_of(d)], q_in.at[there], qsend.at[d], qrecv.at[there], d)

    def result_copy(peer, there):
        return pltpu.make_async_remote_copy(
            src_ref=sent.at[peer],
            dst_ref=arrived.at[there],
            send_sem=rsend.at[peer],
            recv_sem=rrecv.at[there],
            device_id={"group": peer},
            device_id_type=MESH,
        )

    lane = iota(table.shape, 1)
    heard = jnp.full(table.shape, -1, jnp.int32)
    for s in range(SPILL):
        heard = jnp.where(lane == s, request[owned + s], heard)
    table[...] = heard
    table_in[pl.ds(me, 1)] = jnp.full((1,) + table.shape, -1, jnp.int32)
    q_in[pl.ds(me, 1)] = jnp.zeros((1, span, width), BF16)
    loads[0].wait()

    def norm_step(t, c):
        normed[pl.ds(t * rows, rows)] = rms(tokens[t].astype(F32), gain[...]).astype(BF16)
        return c

    lax.fori_loop(0, steps, norm_step, 0)
    pl.semaphore_wait(barrier, groups - 1)
    each_peer(lambda d: table_copy(d, me).start())
    loads[1].wait()
    q = dot_nt(normed[...], wbuf[0]).astype(BF16).astype(F32) * size ** (-0.5)
    q_step[...] = q.astype(BF16).reshape(steps, rows, width)
    q_req[...] = (
        q.reshape(steps, local, BEAMS, width)
        .transpose(1, 0, 2, 3)
        .reshape(local, span, width)
        .astype(BF16)
    )
    each_peer(lambda d: table_copy(d, lax.rem(me + d, groups)).wait_recv())
    batch = 8
    flat = q_req[...].reshape(local * span, width)

    def select_batch(i, c):
        heard = table_in[pl.ds(i * batch, batch)]
        where = jnp.max(
            jnp.where(heard // local == me, heard - me * local, -1), axis=-1, keepdims=True
        )
        rows8 = table_in[pl.ds(i * batch, batch), 0, :]
        where8 = jnp.max(
            jnp.where(rows8 // local == me, rows8 - me * local, -1), axis=-1, keepdims=True
        )
        loc_v[pl.ds(pl.multiple_of(i * batch, batch), batch)] = jnp.broadcast_to(where8, (batch, 128))
        tall = jnp.concatenate([where] * (span // 8), axis=1)
        shape = (batch, span, local * span)
        hit = iota(shape, 2) - iota(shape, 1) == tall * span
        pick = jnp.where(hit, 1.0, 0.0).astype(BF16).reshape(batch * span, local * span)
        send[pl.ds(i * batch, batch)] = dot(pick, flat).astype(BF16).reshape(batch, span, width)
        return c

    lax.fori_loop(0, groups // batch, select_batch, 0)
    each_peer(lambda d: query_copy(d, me).start())
    to_scalar = pltpu.make_async_copy(loc_v, loc, msem.at[0])
    to_scalar.start()

    loads[2].wait()
    k_new[...] = dot_nt(normed[...], wbuf[1]).astype(BF16).reshape(steps, rows, width)
    loads[3].wait()
    v_new[...] = dot_nt(normed[...], wbuf[2]).astype(BF16).reshape(steps, rows, width)
    gate = jax.nn.log_sigmoid(dot_nt(normed[...], wf[...]) + bias[...])
    spread = jnp.where(iota((heads, width), 1) // size == iota((heads, width), 0), 1.0, 0.0)
    f_new[...] = exact_dot(gate, spread).reshape(steps, rows, width)
    dec[...] = decay[...].astype(F32)
    low = iota((span, 128), 1) < 64
    masks = jnp.concatenate([jnp.where(low, 1.0, 0.0), jnp.where(low, 0.0, 1.0)], axis=0).astype(BF16)

    def bias_of(page):
        inside = iota((1, 128), 1) < fill[page]
        return [jnp.where(inside, dec[h, pl.ds(page, 1), :], MASKED) for h in range(heads)]

    for r in range(local):
        last[r] = 0
    for s in range(groups):
        found = jnp.int32(0)
        for i in range(SPILL):
            found = jnp.where(request[owned + i] // local == s, i, found)
        slot[s] = found
    s_numer[0] = jnp.zeros((span, width), F32)
    s_total[0] = jnp.zeros((span, width), F32)
    s_top[0] = jnp.full((span, width), MASKED, F32)

    def chain(r, entry, numer, top, total):
        before = last[jnp.maximum(r, 0)]
        for j in range(blocks):
            cut = slice(128 * j, 128 * (j + 1))
            old = s_top[before, :, cut]
            best = jnp.maximum(old, top[j])
            keep = jnp.exp(old - best)
            add = jnp.exp(top[j] - best)
            s_numer[entry, :, cut] = s_numer[before, :, cut] * keep + numer[j] * add
            s_total[entry, :, cut] = s_total[before, :, cut] * keep + total[j] * add
            s_top[entry, :, cut] = best
        for i in range(local):
            last[i] = jnp.where(r == i, entry, last[i])

    loads[4].wait()
    loads[5].wait()
    unroll = 4

    def own_pages(i, c):
        found = []
        for u in range(unroll):
            page = i * unroll + u
            r = lax.rem(request[page], local)
            found.append(
                (r, page, page_partial(q_req[r], masks, keys.at[page], values.at[page], bias_of(page)))
            )
        for r, page, (numer, top, total, _, _) in found:
            chain(r, page + 1, numer, top, total)
        return c

    lax.fori_loop(0, owned // unroll, own_pages, 0)

    pair = 2

    def hosted(i, c):
        found = []
        for u in range(pair):
            d = i * pair + u
            source = lax.rem(me - d + groups, groups)

            @pl.when(d > 0)
            def _():
                remote(send.at[source], q_in.at[source], qsend.at[0], qrecv.at[source], 1).wait_recv()

        for u in range(pair):
            source = lax.rem(me - (i * pair + u) + groups, groups)
            page = owned + slot[source]
            found.append(
                (source, page_partial(q_in[source], masks, keys.at[page], values.at[page], bias_of(page)))
            )
        for source, (numer, _, _, tops, totals) in found:
            for j in range(blocks):
                sent[source, :, 128 * j : 128 * (j + 1)] = numer[j].astype(BF16)
            sent[source, :, width:] = pack_stats(tops, totals).astype(BF16)
        for u in range(pair):
            d = i * pair + u
            source = lax.rem(me - d + groups, groups)

            @pl.when(d > 0)
            def _():
                result_copy(source, me).start()

        return c

    lax.fori_loop(0, groups // pair, hosted, 0)
    history(q_step, k_new, v_new, f_new, parents, h_numer, h_top, h_total, heads)
    to_scalar.wait()
    shape = (STAT, 2 * width)
    row, col = iota(shape, 0), iota(shape, 1)
    second = jnp.where(col >= width, 1, 0)
    expand = (row // 8 // 3 == second) & (row % 8 == (col - second * width) // size)
    expand = jnp.where(expand, 1.0, 0.0).astype(BF16)

    def absorb(d, c):
        source = peer_of(d)
        result_copy(source, source).wait_recv()
        stats = dot(arrived[source, :, width:], expand)
        cuts = [slice(128 * j, 128 * (j + 1)) for j in range(blocks)]
        numer = [arrived[source, :, cut].astype(F32) for cut in cuts]
        top = [stats[:, cut] for cut in cuts]
        total = [stats[:, width + cut.start : width + cut.stop] for cut in cuts]
        chain(loc[source, 0], owned + d, numer, top, total)
        return c

    lax.fori_loop(1, groups, absorb, 0)

    for r in range(local):
        cut = slice(r * BEAMS, (r + 1) * BEAMS)
        entry = last[r]
        shape = (steps, BEAMS, width)
        p_top = s_top[entry].reshape(shape)
        best = jnp.maximum(p_top, h_top[:, cut])
        p_scale = jnp.exp(p_top - best)
        h_scale = jnp.exp(h_top[:, cut] - best)
        whole = s_total[entry].reshape(shape) * p_scale + h_total[:, cut] * h_scale
        mixed = s_numer[entry].reshape(shape) * p_scale + h_numer[:, cut] * h_scale
        final[:, cut] = mixed / whole
    att[...] = final[...].astype(BF16)

    def finish(d):
        table_copy(d, me).wait_send()
        query_copy(d, me).wait_send()
        result_copy(peer_of(d), me).wait_send()

    each_peer(finish)


def tail_kernel(
    att, tokens, gain, wo_h, wg_h, wu_h, wd_h, out,
    wo, wg, wu, wd, keep, resid, normed, acc,
    a_tx, a_rx, b_tx, b_rx, c_tx, c_rx, d_tx, d_rx,
    wsem, sems_s, sems_r,
):
    steps, rows, model = out.shape
    half = rows // 2
    me = lax.axis_index("head")
    core = lax.rem(me, 2)
    sibling = {"head": me + 1 - 2 * core}
    chip = me // 2
    across = {"head": core + 2 * (1 - chip)}
    mine = pl.ds(pl.multiple_of(core * half, half), half)
    theirs = pl.ds(pl.multiple_of((1 - core) * half, half), half)
    loads = [
        pltpu.make_async_copy(a, b, wsem.at[i])
        for i, (a, b) in enumerate(((wo_h, wo), (wg_h, wg), (wu_h, wu), (wd_h, wd)))
    ]
    for load in loads:
        load.start()
    greet((sibling, across))

    def remote(kind, t, src, dst, device):
        return pltpu.make_async_remote_copy(
            src_ref=src,
            dst_ref=dst,
            send_sem=sems_s.at[kind, t],
            recv_sem=sems_r.at[kind, t],
            device_id=device,
            device_id_type=MESH,
        )

    copy_a = lambda t: remote(0, t, a_tx.at[t], a_rx.at[t], sibling)
    copy_b = lambda t: remote(1, t, b_tx.at[t], b_rx.at[t], across)
    copy_n = lambda t: remote(2, t, normed.at[t, mine], normed.at[t, mine], sibling)
    copy_n_in = lambda t: remote(2, t, normed.at[t, theirs], normed.at[t, theirs], sibling)
    copy_c = lambda t: remote(3, t, c_tx.at[t], c_rx.at[t], sibling)
    copy_d = lambda t: remote(4, t, d_tx.at[t], d_rx.at[t], across)
    copy_o = lambda t: remote(5, t, out.at[t, mine], out.at[t, mine], sibling)
    copy_o_in = lambda t: remote(5, t, out.at[t, theirs], out.at[t, theirs], sibling)

    loads[0].wait()

    def project(t, c):
        acc[...] = dot(att[t], wo[...])
        keep[t] = acc[mine]
        a_tx[t] = acc[theirs].astype(BF16)
        copy_a(t).start()
        return c

    lax.fori_loop(0, steps, project, 0)

    def cross(t, c):
        copy_a(t).wait_recv()
        b_tx[t] = (keep[t] + a_rx[t].astype(F32)).astype(BF16)
        copy_b(t).start()
        return c

    lax.fori_loop(0, steps, cross, 0)
    for load in loads[1:]:
        load.wait()

    def down_cross(t):
        copy_c(t).wait_recv()
        d_tx[t] = (keep[t] + c_rx[t].astype(F32)).astype(BF16)
        copy_d(t).start()

    def feed(t, c):
        copy_b(t).wait_recv()
        res = tokens[t, mine].astype(F32) + (b_tx[t].astype(F32) + b_rx[t].astype(F32))
        resid[t] = res
        normed[t, mine] = rms(res, gain[...]).astype(BF16)
        copy_n(t).start()

        @pl.when(t > 0)
        def _():
            down_cross(t - 1)

        copy_n_in(t).wait_recv()
        x = normed[t]
        gate = dot(x, wg[...])
        up = dot(x, wu[...])
        hidden = (gate / (1.0 + jnp.exp(-gate)) * up).astype(BF16)
        acc[...] = dot(hidden, wd[...])
        keep[t] = acc[mine]
        c_tx[t] = acc[theirs].astype(BF16)
        copy_c(t).start()
        return c

    lax.fori_loop(0, steps, feed, 0)
    down_cross(steps - 1)

    def close(t, c):
        copy_d(t).wait_recv()
        total = resid[t] + (d_tx[t].astype(F32) + d_rx[t].astype(F32))
        out[t, mine] = total.astype(BF16)
        copy_o(t).start()
        return c

    lax.fori_loop(0, steps, close, 0)

    def finish(t, c):
        copy_o_in(t).wait_recv()
        copy_a(t).wait_send()
        copy_b(t).wait_send()
        copy_n(t).wait_send()
        copy_c(t).wait_send()
        copy_d(t).wait_send()
        copy_o(t).wait_send()
        return c

    lax.fori_loop(0, steps, finish, 0)


VM = pl.BlockSpec(memory_space=pltpu.VMEM)
SM = pl.BlockSpec(memory_space=pltpu.SMEM)
HB = pl.BlockSpec(memory_space=pl.ANY)
DMA = pltpu.SemaphoreType.DMA
LIMIT = 60 << 20


def params(**kw):
    return pltpu.CompilerParams(vmem_limit_bytes=LIMIT, **kw)


def shards(
    tokens, parents, page_request, page_fill, keys_pool, values_pool, decay_pool, gain_attn,
    w_query, w_key, w_value, w_forget, forget_bias, w_out, gain_ffn, w_gate, w_up, w_down,
):
    steps, rows, model = tokens.shape
    heads = w_forget.shape[1]
    width = w_query.shape[0]
    local = rows // BEAMS
    span = steps * BEAMS
    groups = lax.axis_size("group")
    pages = page_request.shape[0]
    ff = w_gate.shape[1]
    sds = jax.ShapeDtypeStruct
    block = (steps, rows, width)
    chain = (pages - SPILL + groups, span, width)
    attended = pl.pallas_call(
        functools.partial(group_kernel, groups, local, heads),
        out_shape=sds(block, BF16),
        in_specs=[SM, SM, HB, VM, HB, HB, HB, VM, VM, VM, HB, HB, VM],
        out_specs=VM,
        scratch_shapes=[
            pltpu.VMEM(tokens.shape, BF16),
            pltpu.VMEM((3, width, model), BF16),
            pltpu.VMEM(keys_pool.shape, BF16),
            pltpu.VMEM(values_pool.shape, BF16),
            pltpu.VMEM((heads, pages, 128), F32),
            pltpu.VMEM((steps * rows, model), BF16),
            pltpu.VMEM((local, span, width), BF16),
            pltpu.VMEM(block, BF16),
            pltpu.VMEM(block, BF16),
            pltpu.VMEM(block, BF16),
            pltpu.VMEM(block, F32),
            pltpu.VMEM((8, 128), jnp.int32),
            pltpu.VMEM((groups, 8, 128), jnp.int32),
            pltpu.VMEM((groups, 128), jnp.int32),
            pltpu.VMEM((groups, span, width), BF16),
            pltpu.VMEM((groups, span, width), BF16),
            pltpu.VMEM((groups, span, width + STAT), BF16),
            pltpu.VMEM((groups, span, width + STAT), BF16),
        ]
        + [pltpu.VMEM(chain, F32)] * 3
        + [pltpu.VMEM(block, F32)] * 4
        + [
            pltpu.SMEM((groups, 128), jnp.int32),
            pltpu.SMEM((local,), jnp.int32),
            pltpu.SMEM((groups,), jnp.int32),
            DMA((6,)),
            DMA((1,)),
        ]
        + [DMA((groups,))] * 6,
        compiler_params=params(collective_id=0, has_side_effects=True),
        name="group",
    )(
        page_request, page_fill, tokens, gain_attn, w_query, w_key, w_value, w_forget.T,
        forget_bias[None], parents, keys_pool, values_pool, decay_pool.transpose(1, 0, 2),
    )

    half = (steps, rows // 2, model)
    return pl.pallas_call(
        tail_kernel,
        out_shape=sds((steps, rows, model), BF16),
        in_specs=[VM, VM, VM, HB, HB, HB, HB],
        out_specs=VM,
        scratch_shapes=[
            pltpu.VMEM((width, model), BF16),
            pltpu.VMEM((model, ff), BF16),
            pltpu.VMEM((model, ff), BF16),
            pltpu.VMEM((ff, model), BF16),
            pltpu.VMEM(half, F32),
            pltpu.VMEM(half, F32),
            pltpu.VMEM((steps, rows, model), BF16),
            pltpu.VMEM((rows, model), F32),
        ]
        + [pltpu.VMEM(half, BF16)] * 8
        + [DMA((4,)), DMA((6, steps)), DMA((6, steps))],
        compiler_params=params(collective_id=2, has_side_effects=True),
        name="tail",
    )(attended, tokens, gain_ffn, w_out, w_gate, w_up, w_down)


def solution(mesh):
    return jax.shard_map(
        shards,
        mesh=mesh,
        in_specs=(
            P(None, "group", None),
            P(None, "group"),
            P("group"),
            P("group"),
            P("group", "head", None),
            P("group", "head", None),
            P("group", "head", None),
            P(),
            P("head", None),
            P("head", None),
            P("head", None),
            P(None, "head"),
            P("head"),
            P("head", None),
            P(),
            P(None, "head"),
            P(None, "head"),
            P("head", None),
        ),
        out_specs=P(None, "group", None),
        check_vma=False,
    )
```

```python
import functools

import jax
import jax.numpy as jnp
from jax import lax
from jax.experimental import pallas as pl
from jax.experimental.pallas import tpu as pltpu
from jax.sharding import PartitionSpec as P

BEAMS = 8
OWNED_SLOTS = 32
SPILL = 16
STAT = 128
EPS = 1e-05
MASKED = -1e30
F32 = jnp.float32
BF16 = jnp.bfloat16
MESH = pl.DeviceIdType.MESH


def rms(x, gain):
    return x * lax.rsqrt(jnp.mean(x * x, axis=-1, keepdims=True) + EPS) * gain


def dot(a, b):
    return jnp.dot(a, b, preferred_element_type=F32)


def dot_nt(a, b):
    return lax.dot_general(a, b, (((1,), (1,)), ((), ())), preferred_element_type=F32)


def exact_dot(a, b):
    return jnp.dot(a, b, preferred_element_type=F32, precision=lax.Precision.HIGHEST)


def iota(shape, dim):
    return lax.broadcasted_iota(jnp.int32, shape, dim)


def page_partial(q, masks, keys, values, bias):
    span, width = q.shape
    low = iota((span, 128), 1) < 64
    numer, top, total, tops, totals = [], [], [], [], []
    for j in range(width // 128):
        cut = slice(128 * j, 128 * (j + 1))
        wide = jnp.concatenate([q[:, cut]] * 2, axis=0) * masks
        shift = jnp.concatenate([jnp.broadcast_to(b, (span, 128)) for b in bias[2 * j : 2 * j + 2]], axis=0)
        scores = dot(wide, keys[cut]) + shift
        best = jnp.max(scores, axis=-1, keepdims=True)
        weight = jnp.exp(scores - best)
        whole = jnp.sum(weight, axis=-1, keepdims=True)
        out = dot(weight.astype(BF16), values[cut].astype(F32).T.astype(BF16))
        numer.append(jnp.where(low, out[:span], out[span:]))
        best = jnp.broadcast_to(best, (2 * span, 128))
        whole = jnp.broadcast_to(whole, (2 * span, 128))
        top.append(jnp.where(low, best[:span], best[span:]))
        total.append(jnp.where(low, whole[:span], whole[span:]))
        tops += [best[:span], best[span:]]
        totals += [whole[:span], whole[span:]]
    return numer, top, total, tops, totals


def pack_stats(tops, totals):
    span = tops[0].shape[0]
    lane = iota((span, STAT), 1)
    head, kind = lane % 8, lane // 8
    value = jnp.zeros((span, STAT), F32)
    for h, (a, b) in enumerate(zip(tops, totals)):
        value = jnp.where(head == h, jnp.where(kind < 3, a, b), value)
    first = value.astype(BF16).astype(F32)
    rest = value - first
    second = rest.astype(BF16).astype(F32)
    third = rest - second
    pick = jnp.where(kind < 3, kind, kind - 3)
    out = jnp.where(pick == 0, first, jnp.where(pick == 1, second, third))
    return jnp.where(kind < 6, out, 0.0)


def history(q, k, v, f, parents, numer_out, top_out, total_out, heads):
    steps, rows, width = q.shape
    size = width // heads
    square = (width, width)
    same = jnp.where(iota(square, 0) // size == iota(square, 1) // size, 1.0, 0.0).astype(BF16)
    keys, vals, sums = [], [], []
    for t in range(steps):
        if t > 0:
            lane = iota((rows, rows), 1)
            source = lane - lane % BEAMS + parents[t - 1 : t]
            pick = jnp.where(iota((rows, rows), 0) == source, 1.0, 0.0).T
            pick16 = pick.astype(BF16)
            keys = [dot(pick16, a).astype(BF16) for a in keys]
            vals = [dot(pick16, a).astype(BF16) for a in vals]
            sums = [exact_dot(pick, a) for a in sums]
        keys.append(k[t])
        vals.append(v[t])
        sums.append(f[t] + sums[-1] if t > 0 else f[t])
        asked = q[t].astype(F32)
        scores = []
        for key, total in zip(keys, sums):
            product = asked * key.astype(F32)
            high = product.astype(BF16)
            low = (product - high.astype(F32)).astype(BF16)
            scores.append((dot(high, same) + dot(low, same)) - total)
        best = functools.reduce(jnp.maximum, scores)
        weights = [jnp.exp(s - best) for s in scores]
        top_out[t] = best
        total_out[t] = functools.reduce(jnp.add, weights)
        numer_out[t] = functools.reduce(
            jnp.add, [w.astype(BF16).astype(F32) * a.astype(F32) for w, a in zip(weights, vals)]
        )


def group_kernel(
    groups, local, heads, request, fill, tokens_h, gain, wq, wk, wv, wf, bias, parents, keys_h, values_h, decay,
    wo_h, gain_ffn, wg_h, wu_h, wd_h,
    out,
    att, tokens, wbuf, keys, values, dec, normed, q_req, q_step, k_new, v_new, f_new,
    table, table_in, loc_v, send, q_in, sent, arrived, s_numer, s_top, s_total, h_numer, h_top, h_total, final,
    loc, last, slot,
    lsem, msem, tsend, trecv, qsend, qrecv, rsend, rrecv,
    wo, wg, wu, wd, keep, residual, normed_ffn, acc,
    a_tx, a_rx, b_tx, b_rx, c_tx, c_rx, d_tx, d_rx,
    wsem, sems_s, sems_r,
):
    steps, rows, width = q_step.shape
    span = steps * BEAMS
    pages = keys.shape[0]
    owned = pages - SPILL
    size = width // heads
    blocks = width // 128
    me = lax.axis_index("group")
    half = rows // 2
    head = lax.axis_index("head")
    core = lax.rem(head, 2)
    sibling = {"head": head + 1 - 2 * core}
    across = {"head": core + 2 * (1 - head // 2)}
    wloads = [
        pltpu.make_async_copy(a, b, wsem.at[i])
        for i, (a, b) in enumerate(((wo_h, wo), (wg_h, wg), (wu_h, wu), (wd_h, wd)))
    ]
    loads = [
        pltpu.make_async_copy(a, b, lsem.at[i])
        for i, (a, b) in enumerate(
            (
                (tokens_h, tokens),
                (wq, wbuf.at[0]),
                (wk, wbuf.at[1]),
                (wv, wbuf.at[2]),
                (keys_h, keys),
                (values_h, values),
            )
        )
    ]
    for load in loads[:2]:
        load.start()
    barrier = pltpu.get_barrier_semaphore()

    def peer_of(d):
        return lax.rem(me + d, groups)

    def each_peer(body):
        def step(d, c):
            body(d)
            return c

        lax.fori_loop(1, groups, step, 0)

    each_peer(
        lambda d: pl.semaphore_signal(
            barrier, inc=1, device_id={"group": peer_of(d)}, device_id_type=MESH
        )
    )

    for other in (sibling, across):
        pl.semaphore_signal(barrier, inc=1, device_id=other, device_id_type=MESH)

    def remote(src, dst, ssem, rsem, d):
        return pltpu.make_async_remote_copy(
            src_ref=src,
            dst_ref=dst,
            send_sem=ssem,
            recv_sem=rsem,
            device_id={"group": peer_of(d)},
            device_id_type=MESH,
        )

    def table_copy(d, there):
        return remote(table, table_in.at[there], tsend.at[d], trecv.at[there], d)

    def query_copy(d, there):
        return remote(send.at[peer_of(d)], q_in.at[there], qsend.at[d], qrecv.at[there], d)

    def result_copy(peer, there):
        return pltpu.make_async_remote_copy(
            src_ref=sent.at[peer],
            dst_ref=arrived.at[there],
            send_sem=rsend.at[peer],
            recv_sem=rrecv.at[there],
            device_id={"group": peer},
            device_id_type=MESH,
        )

    lane = iota(table.shape, 1)
    heard = jnp.full(table.shape, -1, jnp.int32)
    for s in range(SPILL):
        heard = jnp.where(lane == s, request[owned + s], heard)
    table[...] = heard
    table_in[pl.ds(me, 1)] = jnp.full((1,) + table.shape, -1, jnp.int32)
    q_in[pl.ds(me, 1)] = jnp.zeros((1, span, width), BF16)
    pl.semaphore_wait(barrier, groups + 1)
    each_peer(lambda d: table_copy(d, me).start())
    loads[0].wait()

    def norm_step(t, c):
        normed[pl.ds(t * rows, rows)] = rms(tokens[t].astype(F32), gain[...]).astype(BF16)
        return c

    lax.fori_loop(0, steps, norm_step, 0)
    for load in loads[2:] + wloads:
        load.start()
    each_peer(lambda d: table_copy(d, lax.rem(me + d, groups)).wait_recv())
    batch = 8
    for i in range(groups // batch):
        heard = table_in[i * batch : (i + 1) * batch, 0, :]
        where = jnp.max(
            jnp.where(heard // local == me, heard - me * local, -1), axis=-1, keepdims=True
        )
        loc_v[i * batch : (i + 1) * batch] = jnp.broadcast_to(where, (batch, 128))
    to_scalar = pltpu.make_async_copy(loc_v, loc, msem.at[0])
    to_scalar.start()
    loads[1].wait()
    q = dot_nt(normed[...], wbuf[0]).astype(BF16).astype(F32) * size ** (-0.5)
    q_req[...] = (
        q.reshape(steps, local, BEAMS, width)
        .transpose(1, 0, 2, 3)
        .reshape(local, span, width)
        .astype(BF16)
    )
    to_scalar.wait()

    def send_query(d):
        peer = peer_of(d)
        send[peer] = q_req[jnp.maximum(loc[peer, 0], 0)]
        query_copy(d, me).start()

    each_peer(send_query)
    q_step[...] = q.astype(BF16).reshape(steps, rows, width)

    loads[2].wait()
    k_new[...] = dot_nt(normed[...], wbuf[1]).astype(BF16).reshape(steps, rows, width)
    loads[3].wait()
    v_new[...] = dot_nt(normed[...], wbuf[2]).astype(BF16).reshape(steps, rows, width)
    gate = jax.nn.log_sigmoid(dot_nt(normed[...], wf[...]) + bias[...])
    spread = jnp.where(iota((heads, width), 1) // size == iota((heads, width), 0), 1.0, 0.0)
    f_new[...] = exact_dot(gate, spread).reshape(steps, rows, width)
    dec[...] = decay[...].astype(F32)
    low = iota((span, 128), 1) < 64
    masks = jnp.concatenate([jnp.where(low, 1.0, 0.0), jnp.where(low, 0.0, 1.0)], axis=0).astype(BF16)

    def bias_of(page):
        inside = iota((1, 128), 1) < fill[page]
        return [jnp.where(inside, dec[h, pl.ds(page, 1), :], MASKED) for h in range(heads)]

    for r in range(local):
        last[r] = 0
    for s in range(groups):
        found = jnp.int32(0)
        for i in range(SPILL):
            found = jnp.where(request[owned + i] // local == s, i, found)
        slot[s] = found
    s_numer[0] = jnp.zeros((span, width), F32)
    s_total[0] = jnp.zeros((span, width), F32)
    s_top[0] = jnp.full((span, width), MASKED, F32)

    def chain(r, entry, numer, top, total):
        before = last[jnp.maximum(r, 0)]
        for j in range(blocks):
            cut = slice(128 * j, 128 * (j + 1))
            old = s_top[before, :, cut]
            best = jnp.maximum(old, top[j])
            keep = jnp.exp(old - best)
            add = jnp.exp(top[j] - best)
            s_numer[entry, :, cut] = s_numer[before, :, cut] * keep + numer[j] * add
            s_total[entry, :, cut] = s_total[before, :, cut] * keep + total[j] * add
            s_top[entry, :, cut] = best
        for i in range(local):
            last[i] = jnp.where(r == i, entry, last[i])

    loads[4].wait()
    loads[5].wait()
    history(q_step, k_new, v_new, f_new, parents, h_numer, h_top, h_total, heads)
    pair = 2

    def hosted(i, c):
        found = []
        for u in range(pair):
            d = i * pair + u
            source = lax.rem(me - d + groups, groups)

            @pl.when(d > 0)
            def _():
                remote(send.at[source], q_in.at[source], qsend.at[0], qrecv.at[source], 1).wait_recv()

        for u in range(pair):
            source = lax.rem(me - (i * pair + u) + groups, groups)
            page = owned + slot[source]
            found.append(
                (source, page_partial(q_in[source], masks, keys.at[page], values.at[page], bias_of(page)))
            )
        for source, (numer, _, _, tops, totals) in found:
            for j in range(blocks):
                sent[source, :, 128 * j : 128 * (j + 1)] = numer[j].astype(BF16)
            sent[source, :, width:] = pack_stats(tops, totals).astype(BF16)
        for u in range(pair):
            d = i * pair + u
            source = lax.rem(me - d + groups, groups)

            @pl.when(d > 0)
            def _():
                result_copy(source, me).start()

        return c

    lax.fori_loop(0, groups // pair, hosted, 0)
    unroll = 4

    def own_pages(i, c):
        found = []
        for u in range(unroll):
            page = i * unroll + u
            r = lax.rem(request[page], local)
            found.append(
                (r, page, page_partial(q_req[r], masks, keys.at[page], values.at[page], bias_of(page)))
            )
        for r, page, (numer, top, total, _, _) in found:
            chain(r, page + 1, numer, top, total)
        return c

    lax.fori_loop(0, owned // unroll, own_pages, 0)

    shape = (STAT, 2 * width)
    row, col = iota(shape, 0), iota(shape, 1)
    second = jnp.where(col >= width, 1, 0)
    expand = (row // 8 // 3 == second) & (row % 8 == (col - second * width) // size)
    expand = jnp.where(expand, 1.0, 0.0).astype(BF16)

    def absorb(d, c):
        source = peer_of(d)
        result_copy(source, source).wait_recv()
        stats = dot(arrived[source, :, width:], expand)
        cuts = [slice(128 * j, 128 * (j + 1)) for j in range(blocks)]
        numer = [arrived[source, :, cut].astype(F32) for cut in cuts]
        top = [stats[:, cut] for cut in cuts]
        total = [stats[:, width + cut.start : width + cut.stop] for cut in cuts]
        chain(loc[source, 0], owned + d, numer, top, total)
        return c

    lax.fori_loop(1, groups, absorb, 0)

    for r in range(local):
        cut = slice(r * BEAMS, (r + 1) * BEAMS)
        entry = last[r]
        shape = (steps, BEAMS, width)
        p_top = s_top[entry].reshape(shape)
        best = jnp.maximum(p_top, h_top[:, cut])
        p_scale = jnp.exp(p_top - best)
        h_scale = jnp.exp(h_top[:, cut] - best)
        whole = s_total[entry].reshape(shape) * p_scale + h_total[:, cut] * h_scale
        mixed = s_numer[entry].reshape(shape) * p_scale + h_numer[:, cut] * h_scale
        final[:, cut] = mixed / whole
    att[...] = final[...].astype(BF16)

    def finish(d):
        table_copy(d, me).wait_send()
        query_copy(d, me).wait_send()
        result_copy(peer_of(d), me).wait_send()

    each_peer(finish)

    mine = pl.ds(pl.multiple_of(core * half, half), half)
    theirs = pl.ds(pl.multiple_of((1 - core) * half, half), half)
    def pair_copy(kind, t, src, dst, device):
        return pltpu.make_async_remote_copy(
            src_ref=src,
            dst_ref=dst,
            send_sem=sems_s.at[kind, t],
            recv_sem=sems_r.at[kind, t],
            device_id=device,
            device_id_type=MESH,
        )

    copy_a = lambda t: pair_copy(0, t, a_tx.at[t], a_rx.at[t], sibling)
    copy_b = lambda t: pair_copy(1, t, b_tx.at[t], b_rx.at[t], across)
    copy_n = lambda t: pair_copy(2, t, normed_ffn.at[t, mine], normed_ffn.at[t, mine], sibling)
    copy_n_in = lambda t: pair_copy(2, t, normed_ffn.at[t, theirs], normed_ffn.at[t, theirs], sibling)
    copy_c = lambda t: pair_copy(3, t, c_tx.at[t], c_rx.at[t], sibling)
    copy_d = lambda t: pair_copy(4, t, d_tx.at[t], d_rx.at[t], across)
    copy_o = lambda t: pair_copy(5, t, out.at[t, mine], out.at[t, mine], sibling)
    copy_o_in = lambda t: pair_copy(5, t, out.at[t, theirs], out.at[t, theirs], sibling)

    wloads[0].wait()

    def project(t):
        acc[...] = dot(att[t], wo[...])
        keep[t] = acc[mine]
        a_tx[t] = acc[theirs].astype(BF16)
        copy_a(t).start()

    def cross(t):
        copy_a(t).wait_recv()
        b_tx[t] = (keep[t] + a_rx[t].astype(F32)).astype(BF16)
        copy_b(t).start()

    def lead(t, c):
        @pl.when(t < steps)
        def _():
            project(t)

        @pl.when(t > 0)
        def _():
            cross(t - 1)

        return c

    lax.fori_loop(0, steps + 1, lead, 0)
    for load in wloads[1:]:
        load.wait()

    def down_cross(t):
        copy_c(t).wait_recv()
        d_tx[t] = (keep[t] + c_rx[t].astype(F32)).astype(BF16)
        copy_d(t).start()

    def feed(t, c):
        copy_b(t).wait_recv()
        res = tokens[t, mine].astype(F32) + (b_tx[t].astype(F32) + b_rx[t].astype(F32))
        residual[t] = res
        normed_ffn[t, mine] = rms(res, gain_ffn[...]).astype(BF16)
        copy_n(t).start()

        @pl.when(t > 0)
        def _():
            down_cross(t - 1)

        copy_n_in(t).wait_recv()
        x = normed_ffn[t]
        gate = dot(x, wg[...])
        up = dot(x, wu[...])
        hidden = (gate / (1.0 + jnp.exp(-gate)) * up).astype(BF16)
        acc[...] = dot(hidden, wd[...])
        keep[t] = acc[mine]
        c_tx[t] = acc[theirs].astype(BF16)
        copy_c(t).start()
        return c

    lax.fori_loop(0, steps, feed, 0)
    down_cross(steps - 1)

    def emit(t, c):
        copy_d(t).wait_recv()
        total = residual[t] + (d_tx[t].astype(F32) + d_rx[t].astype(F32))
        out[t, mine] = total.astype(BF16)
        copy_o(t).start()
        return c

    lax.fori_loop(0, steps, emit, 0)

    def settle(t, c):
        copy_o_in(t).wait_recv()
        copy_a(t).wait_send()
        copy_b(t).wait_send()
        copy_n(t).wait_send()
        copy_c(t).wait_send()
        copy_d(t).wait_send()
        copy_o(t).wait_send()
        return c

    lax.fori_loop(0, steps, settle, 0)


VM = pl.BlockSpec(memory_space=pltpu.VMEM)
SM = pl.BlockSpec(memory_space=pltpu.SMEM)
HB = pl.BlockSpec(memory_space=pl.ANY)
DMA = pltpu.SemaphoreType.DMA
LIMIT = 60 << 20


def params(**kw):
    return pltpu.CompilerParams(vmem_limit_bytes=LIMIT, **kw)


def shards(
    tokens, parents, page_request, page_fill, keys_pool, values_pool, decay_pool, gain_attn,
    w_query, w_key, w_value, w_forget, forget_bias, w_out, gain_ffn, w_gate, w_up, w_down,
):
    steps, rows, model = tokens.shape
    heads = w_forget.shape[1]
    width = w_query.shape[0]
    local = rows // BEAMS
    span = steps * BEAMS
    groups = lax.axis_size("group")
    pages = page_request.shape[0]
    ff = w_gate.shape[1]
    sds = jax.ShapeDtypeStruct
    block = (steps, rows, width)
    chain = (pages - SPILL + groups, span, width)
    half = (steps, rows // 2, model)
    return pl.pallas_call(
        functools.partial(group_kernel, groups, local, heads),
        out_shape=sds(tokens.shape, BF16),
        in_specs=[SM, SM, HB, VM, HB, HB, HB, VM, VM, VM, HB, HB, VM, HB, VM, HB, HB, HB],
        out_specs=VM,
        scratch_shapes=[
            pltpu.VMEM(block, BF16),
            pltpu.VMEM(tokens.shape, BF16),
            pltpu.VMEM((3, width, model), BF16),
            pltpu.VMEM(keys_pool.shape, BF16),
            pltpu.VMEM(values_pool.shape, BF16),
            pltpu.VMEM((heads, pages, 128), F32),
            pltpu.VMEM((steps * rows, model), BF16),
            pltpu.VMEM((local, span, width), BF16),
            pltpu.VMEM(block, BF16),
            pltpu.VMEM(block, BF16),
            pltpu.VMEM(block, BF16),
            pltpu.VMEM(block, F32),
            pltpu.VMEM((8, 128), jnp.int32),
            pltpu.VMEM((groups, 8, 128), jnp.int32),
            pltpu.VMEM((groups, 128), jnp.int32),
            pltpu.VMEM((groups, span, width), BF16),
            pltpu.VMEM((groups, span, width), BF16),
            pltpu.VMEM((groups, span, width + STAT), BF16),
            pltpu.VMEM((groups, span, width + STAT), BF16),
        ]
        + [pltpu.VMEM(chain, F32)] * 3
        + [pltpu.VMEM(block, F32)] * 4
        + [
            pltpu.SMEM((groups, 128), jnp.int32),
            pltpu.SMEM((local,), jnp.int32),
            pltpu.SMEM((groups,), jnp.int32),
            DMA((6,)),
            DMA((1,)),
        ]
        + [DMA((groups,))] * 6
        + [
            pltpu.VMEM((width, model), BF16),
            pltpu.VMEM((model, ff), BF16),
            pltpu.VMEM((model, ff), BF16),
            pltpu.VMEM((ff, model), BF16),
            pltpu.VMEM(half, F32),
            pltpu.VMEM(half, F32),
            pltpu.VMEM(tokens.shape, BF16),
            pltpu.VMEM((rows, model), F32),
        ]
        + [pltpu.VMEM(half, BF16)] * 8
        + [DMA((4,)), DMA((6, steps)), DMA((6, steps))],
        compiler_params=params(collective_id=0, has_side_effects=True),
        name="layer",
    )(
        page_request, page_fill, tokens, gain_attn, w_query, w_key, w_value, w_forget.T,
        forget_bias[None], parents, keys_pool, values_pool, decay_pool.transpose(1, 0, 2),
        w_out, gain_ffn, w_gate, w_up, w_down,
    )


def solution(mesh):
    return jax.shard_map(
        shards,
        mesh=mesh,
        in_specs=(
            P(None, "group", None),
            P(None, "group"),
            P("group"),
            P("group"),
            P("group", "head", None),
            P("group", "head", None),
            P("group", "head", None),
            P(),
            P("head", None),
            P("head", None),
            P("head", None),
            P(None, "head"),
            P("head"),
            P("head", None),
            P(),
            P(None, "head"),
            P(None, "head"),
            P("head", None),
        ),
        out_specs=P(None, "group", None),
        check_vma=False,
    )
```

```python
import functools

import jax
import jax.numpy as jnp
from jax import lax
from jax.experimental import pallas as pl
from jax.experimental.pallas import tpu as pltpu
from jax.sharding import PartitionSpec as P

BEAMS = 8
OWNED_SLOTS = 32
SPILL = 16
STAT = 128
EPS = 1e-05
MASKED = -1e30
F32 = jnp.float32
BF16 = jnp.bfloat16
MESH = pl.DeviceIdType.MESH


def rms(x, gain):
    return x * lax.rsqrt(jnp.mean(x * x, axis=-1, keepdims=True) + EPS) * gain


def dot(a, b):
    return jnp.dot(a, b, preferred_element_type=F32)


def dot_nt(a, b):
    return lax.dot_general(a, b, (((1,), (1,)), ((), ())), preferred_element_type=F32)


def exact_dot(a, b):
    return jnp.dot(a, b, preferred_element_type=F32, precision=lax.Precision.HIGHEST)


def iota(shape, dim):
    return lax.broadcasted_iota(jnp.int32, shape, dim)


def turn(values):
    return values.astype(F32).T.astype(BF16)


def page_partial(q, masks, keys, values, bias):
    span, width = q.shape
    low = iota((span, 128), 1) < 64
    numer, top, total, tops, totals = [], [], [], [], []
    for j in range(width // 128):
        cut = slice(128 * j, 128 * (j + 1))
        wide = jnp.concatenate([q[:, cut]] * 2, axis=0) * masks
        shift = jnp.concatenate([jnp.broadcast_to(b, (span, 128)) for b in bias[2 * j : 2 * j + 2]], axis=0)
        scores = dot(wide, keys[cut]) + shift
        best = jnp.max(scores, axis=-1, keepdims=True)
        weight = jnp.exp(scores - best)
        whole = jnp.sum(weight, axis=-1, keepdims=True)
        out = dot(weight.astype(BF16), values[:, cut])
        numer.append(jnp.where(low, out[:span], out[span:]))
        best = jnp.broadcast_to(best, (2 * span, 128))
        whole = jnp.broadcast_to(whole, (2 * span, 128))
        top.append(jnp.where(low, best[:span], best[span:]))
        total.append(jnp.where(low, whole[:span], whole[span:]))
        tops += [best[:span], best[span:]]
        totals += [whole[:span], whole[span:]]
    return numer, top, total, tops, totals


def stat_lanes(shape, dim, heads):
    lane = iota(shape, dim)
    place = lane % 32
    return lane // 32, place % heads, place // heads


def pack_stats(tops, totals):
    heads = len(tops)
    quarter = tops[0].shape[0] // 4
    group, head, part = stat_lanes((quarter, STAT), 1, heads)
    value = jnp.zeros((quarter, STAT), F32)
    for g in range(4):
        cut = slice(g * quarter, (g + 1) * quarter)
        for h in range(heads):
            both = jnp.where(part < 3, tops[h][cut], totals[h][cut])
            value = jnp.where((group == g) & (head == h), both, value)
    first = value.astype(BF16).astype(F32)
    rest = value - first
    second = rest.astype(BF16).astype(F32)
    out = jnp.where(part % 3 == 0, first, jnp.where(part % 3 == 1, second, rest - second))
    return jnp.where(part < 5, out, 0.0)


def history(q, k, v, f, parents, numer_out, top_out, total_out, heads):
    steps, rows, width = q.shape
    size = width // heads
    square = (width, width)
    same = jnp.where(iota(square, 0) // size == iota(square, 1) // size, 1.0, 0.0).astype(BF16)
    keys, vals, sums = [], [], []
    for t in range(steps):
        if t > 0:
            lane = iota((rows, rows), 1)
            source = lane - lane % BEAMS + parents[t - 1 : t]
            pick = jnp.where(iota((rows, rows), 0) == source, 1.0, 0.0).T
            pick16 = pick.astype(BF16)
            keys = [dot(pick16, a).astype(BF16) for a in keys]
            vals = [dot(pick16, a).astype(BF16) for a in vals]
            sums = [exact_dot(pick, a) for a in sums]
        keys.append(k[t])
        vals.append(v[t])
        sums.append(f[t] + sums[-1] if t > 0 else f[t])
        asked = q[t].astype(F32)
        scores = []
        for key, total in zip(keys, sums):
            product = asked * key.astype(F32)
            high = product.astype(BF16)
            low = (product - high.astype(F32)).astype(BF16)
            scores.append((dot(high, same) + dot(low, same)) - total)
        best = functools.reduce(jnp.maximum, scores)
        weights = [jnp.exp(s - best) for s in scores]
        top_out[t] = best
        total_out[t] = functools.reduce(jnp.add, weights)
        numer_out[t] = functools.reduce(
            jnp.add, [w.astype(BF16).astype(F32) * a.astype(F32) for w, a in zip(weights, vals)]
        )


def group_kernel(
    groups, local, heads, request, fill, tokens_h, gain, wq, wk, wv, wf, bias, parents, keys_h, values_h, decay,
    wo_h, gain_ffn, wg_h, wu_h, wd_h,
    result,
    out, att, tokens, wbuf, keys, values, dec, normed, q_req, q_step, k_new, v_new, f_new,
    table, table_in, loc_v, send, q_in, sent, arrived, s_numer, s_top, s_total, h_numer, h_top, h_total, final,
    turned,
    loc, last, slot,
    lsem, msem, tsend, trecv, qsend, qrecv, rsend, rrecv,
    wo, wg, wu, wd, keep, residual, acc,
    a_tx, a_rx, b_tx, b_rx, c_tx, c_rx, d_tx, d_rx,
    wsem, osem, sems_s, sems_r,
):
    steps, rows, width = q_step.shape
    span = steps * BEAMS
    pages = keys.shape[0]
    owned = pages - SPILL
    size = width // heads
    blocks = width // 128
    me = lax.axis_index("group")
    half = rows // 2
    head = lax.axis_index("head")
    core = lax.rem(head, 2)
    sibling = {"head": head + 1 - 2 * core}
    across = {"head": core + 2 * (1 - head // 2)}
    wloads = [
        pltpu.make_async_copy(a, b, wsem.at[i])
        for i, (a, b) in enumerate(((wo_h, wo), (wg_h, wg), (wu_h, wu), (wd_h, wd)))
    ]
    loads = [
        pltpu.make_async_copy(a, b, lsem.at[i])
        for i, (a, b) in enumerate(
            (
                (tokens_h, tokens),
                (wq, wbuf.at[0]),
                (wk, wbuf.at[1]),
                (wv, wbuf.at[2]),
                (keys_h, keys),
                (values_h, values),
            )
        )
    ]
    for load in loads[:2]:
        load.start()
    barrier = pltpu.get_barrier_semaphore()

    def peer_of(d):
        return lax.rem(me + d, groups)

    def each_peer(body):
        def step(d, c):
            body(d)
            return c

        lax.fori_loop(1, groups, step, 0)

    each_peer(
        lambda d: pl.semaphore_signal(
            barrier, inc=1, device_id={"group": peer_of(d)}, device_id_type=MESH
        )
    )

    for other in (sibling, across):
        pl.semaphore_signal(barrier, inc=1, device_id=other, device_id_type=MESH)

    def remote(src, dst, ssem, rsem, d):
        return pltpu.make_async_remote_copy(
            src_ref=src,
            dst_ref=dst,
            send_sem=ssem,
            recv_sem=rsem,
            device_id={"group": peer_of(d)},
            device_id_type=MESH,
        )

    def table_copy(d, there):
        return remote(table, table_in.at[there], tsend.at[d], trecv.at[there], d)

    def query_copy(d, there):
        return remote(send.at[peer_of(d)], q_in.at[there], qsend.at[d], qrecv.at[there], d)

    def result_copy(peer, there):
        return pltpu.make_async_remote_copy(
            src_ref=sent.at[peer],
            dst_ref=arrived.at[there],
            send_sem=rsend.at[peer],
            recv_sem=rrecv.at[there],
            device_id={"group": peer},
            device_id_type=MESH,
        )

    lane = iota(table.shape, 1)
    heard = jnp.full(table.shape, -1, jnp.int32)
    for s in range(SPILL):
        heard = jnp.where(lane == s, request[owned + s], heard)
    table[...] = heard
    table_in[pl.ds(me, 1)] = jnp.full((1,) + table.shape, -1, jnp.int32)
    q_in[pl.ds(me, 1)] = jnp.zeros((1, span, width), BF16)
    arrived[pl.ds(me, 1)] = jnp.zeros((1,) + arrived.shape[1:], BF16)
    pl.semaphore_wait(barrier, groups + 1)
    each_peer(lambda d: table_copy(d, me).start())
    loads[0].wait()

    def norm_step(t, c):
        normed[t] = rms(tokens[t].astype(F32), gain[...]).astype(BF16)
        return c

    lax.fori_loop(0, steps, norm_step, 0)
    for load in loads[2:] + wloads:
        load.start()
    each_peer(lambda d: table_copy(d, lax.rem(me + d, groups)).wait_recv())
    batch = 8
    for i in range(groups // batch):
        heard = table_in[i * batch : (i + 1) * batch, 0, :]
        where = jnp.max(
            jnp.where(heard // local == me, heard - me * local, -1), axis=-1, keepdims=True
        )
        loc_v[i * batch : (i + 1) * batch] = jnp.broadcast_to(where, (batch, 128))
    to_scalar = pltpu.make_async_copy(loc_v, loc, msem.at[0])
    to_scalar.start()
    loads[1].wait()
    q = dot_nt(normed[...].reshape(steps * rows, normed.shape[-1]), wbuf[0]).astype(BF16).astype(F32) * size ** (-0.5)
    q_req[...] = (
        q.reshape(steps, local, BEAMS, width)
        .transpose(1, 0, 2, 3)
        .reshape(local, span, width)
        .astype(BF16)
    )
    to_scalar.wait()

    def send_query(d):
        peer = peer_of(d)
        send[peer] = q_req[jnp.maximum(loc[peer, 0], 0)]
        query_copy(d, me).start()

    each_peer(send_query)
    q_step[...] = q.astype(BF16).reshape(steps, rows, width)

    loads[2].wait()
    k_new[...] = dot_nt(normed[...].reshape(steps * rows, normed.shape[-1]), wbuf[1]).astype(BF16).reshape(steps, rows, width)
    loads[3].wait()
    v_new[...] = dot_nt(normed[...].reshape(steps * rows, normed.shape[-1]), wbuf[2]).astype(BF16).reshape(steps, rows, width)
    gate = jax.nn.log_sigmoid(dot_nt(normed[...].reshape(steps * rows, normed.shape[-1]), wf[...]) + bias[...])
    spread = jnp.where(iota((heads, width), 1) // size == iota((heads, width), 0), 1.0, 0.0)
    f_new[...] = exact_dot(gate, spread).reshape(steps, rows, width)
    dec[...] = decay[...].astype(F32)
    low = iota((span, 128), 1) < 64
    masks = jnp.concatenate([jnp.where(low, 1.0, 0.0), jnp.where(low, 0.0, 1.0)], axis=0).astype(BF16)

    def bias_of(page):
        inside = iota((1, 128), 1) < fill[page]
        return [jnp.where(inside, dec[h, pl.ds(page, 1), :], MASKED) for h in range(heads)]

    for r in range(local):
        last[r] = 0
    for s in range(groups):
        found = jnp.int32(0)
        for i in range(SPILL):
            found = jnp.where(request[owned + i] // local == s, i, found)
        slot[s] = found
    s_numer[0] = jnp.zeros((span, width), F32)
    s_total[0] = jnp.zeros((span, width), F32)
    s_top[0] = jnp.full((span, width), MASKED, F32)

    def chain(r, entry, numer, top, total):
        before = last[jnp.maximum(r, 0)]
        for j in range(blocks):
            cut = slice(128 * j, 128 * (j + 1))
            old = s_top[before, :, cut]
            best = jnp.maximum(old, top[j])
            keep = jnp.exp(old - best)
            add = jnp.exp(top[j] - best)
            s_numer[entry, :, cut] = s_numer[before, :, cut] * keep + numer[j] * add
            s_total[entry, :, cut] = s_total[before, :, cut] * keep + total[j] * add
            s_top[entry, :, cut] = best
        for i in range(local):
            last[i] = jnp.where(r == i, entry, last[i])

    loads[4].wait()
    loads[5].wait()
    history(q_step, k_new, v_new, f_new, parents, h_numer, h_top, h_total, heads)
    def turn_page(i, c):
        turned[i] = turn(values[owned + i])
        return c

    lax.fori_loop(0, SPILL, turn_page, 0)

    pair = 4

    def hosted(i, c):
        found = []
        for u in range(pair):
            d = i * pair + u
            source = lax.rem(me - d + groups, groups)

            @pl.when(d > 0)
            def _():
                remote(send.at[source], q_in.at[source], qsend.at[0], qrecv.at[source], 1).wait_recv()

        for u in range(pair):
            source = lax.rem(me - (i * pair + u) + groups, groups)
            page = owned + slot[source]
            found.append(
                (source, page_partial(q_in[source], masks, keys.at[page], turned.at[slot[source]], bias_of(page)))
            )
        for source, (numer, _, _, tops, totals) in found:
            for j in range(blocks):
                sent[source, span * j : span * (j + 1)] = numer[j].astype(BF16)
            sent[source, span * blocks :] = pack_stats(tops, totals).astype(BF16)
        for u in range(pair):
            d = i * pair + u
            source = lax.rem(me - d + groups, groups)

            @pl.when(d > 0)
            def _():
                result_copy(source, me).start()

        return c

    lax.fori_loop(0, groups // pair, hosted, 0)
    unroll = 4

    def own_pages(i, c):
        found = []
        for u in range(unroll):
            page = i * unroll + u
            r = lax.rem(request[page], local)
            found.append(
                (r, page, page_partial(q_req[r], masks, keys.at[page], turn(values[page]), bias_of(page)))
            )
        for r, page, (numer, top, total, _, _) in found:
            chain(r, page + 1, numer, top, total)
        return c

    lax.fori_loop(0, owned // unroll, own_pages, 0)

    shape = (STAT, 2 * width)
    _, row_head, row_part = stat_lanes(shape, 0, heads)
    col = iota(shape, 1)
    is_total = jnp.where(col >= width, 1, 0)
    expand = (row_part // 3 == is_total) & (row_part < 5) & (row_head == (col - is_total * width) // size)
    expand = jnp.where(expand, 1.0, 0.0).astype(BF16)
    owner, _, _ = stat_lanes((span // 4, STAT), 1, heads)

    four = 4

    def absorb(i, c):
        found = []
        for u in range(four):
            d = i * four + u
            source = peer_of(d)

            @pl.when(d > 0)
            def _():
                result_copy(source, source).wait_recv()

            packed = arrived[source, span * blocks :].astype(F32)
            spread_rows = [jnp.where(owner == g, packed, 0.0) for g in range(4)]
            found.append(jnp.concatenate(spread_rows, axis=0).astype(BF16))
        stats = dot(jnp.concatenate(found, axis=0), expand)
        for u in range(four):
            d = i * four + u
            source = peer_of(d)
            part = stats[span * u : span * (u + 1)]
            cuts = [slice(128 * j, 128 * (j + 1)) for j in range(blocks)]
            numer = [arrived[source, span * j : span * (j + 1)].astype(F32) for j in range(blocks)]
            top = [part[:, cut] for cut in cuts]
            total = [part[:, width + cut.start : width + cut.stop] for cut in cuts]
            chain(loc[source, 0], owned + 1 + d, numer, top, total)
        return c

    lax.fori_loop(0, groups // four, absorb, 0)

    for r in range(local):
        cut = slice(r * BEAMS, (r + 1) * BEAMS)
        entry = last[r]
        shape = (steps, BEAMS, width)
        p_top = s_top[entry].reshape(shape)
        best = jnp.maximum(p_top, h_top[:, cut])
        p_scale = jnp.exp(p_top - best)
        h_scale = jnp.exp(h_top[:, cut] - best)
        whole = s_total[entry].reshape(shape) * p_scale + h_total[:, cut] * h_scale
        mixed = s_numer[entry].reshape(shape) * p_scale + h_numer[:, cut] * h_scale
        final[:, cut] = mixed / whole
    att[...] = final[...].astype(BF16)

    def finish(d):
        table_copy(d, me).wait_send()
        query_copy(d, me).wait_send()
        result_copy(peer_of(d), me).wait_send()


    mine = pl.ds(pl.multiple_of(core * half, half), half)
    theirs = pl.ds(pl.multiple_of((1 - core) * half, half), half)
    def pair_copy(kind, t, src, dst, device):
        return pltpu.make_async_remote_copy(
            src_ref=src,
            dst_ref=dst,
            send_sem=sems_s.at[kind, t],
            recv_sem=sems_r.at[kind, t],
            device_id=device,
            device_id_type=MESH,
        )

    copy_a = lambda t: pair_copy(0, t, a_tx.at[t], a_rx.at[t], sibling)
    copy_b = lambda t: pair_copy(1, t, b_tx.at[t], b_rx.at[t], across)
    copy_n = lambda t: pair_copy(2, t, normed.at[t, mine], normed.at[t, mine], sibling)
    copy_n_in = lambda t: pair_copy(2, t, normed.at[t, theirs], normed.at[t, theirs], sibling)
    copy_c = lambda t: pair_copy(3, t, c_tx.at[t], c_rx.at[t], sibling)
    copy_d = lambda t: pair_copy(4, t, d_tx.at[t], d_rx.at[t], across)
    copy_o = lambda t: pair_copy(5, t, out.at[t, mine], out.at[t, mine], sibling)
    copy_o_in = lambda t: pair_copy(5, t, out.at[t, theirs], out.at[t, theirs], sibling)

    wloads[0].wait()

    def project(t):
        acc[...] = dot(att[t], wo[...])
        keep[t] = acc[mine]
        a_tx[t] = acc[theirs].astype(BF16)
        copy_a(t).start()

    def cross(t):
        copy_a(t).wait_recv()
        b_tx[t] = (keep[t] + a_rx[t].astype(F32)).astype(BF16)
        copy_b(t).start()

    def lead(t, c):
        @pl.when(t < steps)
        def _():
            project(t)

        @pl.when(t > 0)
        def _():
            cross(t - 1)

        return c

    lax.fori_loop(0, steps + 1, lead, 0)
    each_peer(finish)
    for load in wloads[1:]:
        load.wait()

    def down_cross(t):
        copy_c(t).wait_recv()
        d_tx[t] = (keep[t] + c_rx[t].astype(F32)).astype(BF16)
        copy_d(t).start()

    def feed(t, c):
        copy_b(t).wait_recv()
        res = tokens[t, mine].astype(F32) + (b_tx[t].astype(F32) + b_rx[t].astype(F32))
        residual[t] = res
        normed[t, mine] = rms(res, gain_ffn[...]).astype(BF16)
        copy_n(t).start()

        @pl.when(t > 0)
        def _():
            down_cross(t - 1)

        copy_n_in(t).wait_recv()
        x = normed[t]
        gate = dot(x, wg[...])
        up = dot(x, wu[...])
        hidden = (gate / (1.0 + jnp.exp(-gate)) * up).astype(BF16)
        acc[...] = dot(hidden, wd[...])
        keep[t] = acc[mine]
        c_tx[t] = acc[theirs].astype(BF16)
        copy_c(t).start()
        return c

    lax.fori_loop(0, steps, feed, 0)
    down_cross(steps - 1)

    def emit(t, c):
        copy_d(t).wait_recv()
        total = residual[t] + (d_tx[t].astype(F32) + d_rx[t].astype(F32))
        out[t, mine] = total.astype(BF16)
        copy_o(t).start()
        return c

    lax.fori_loop(0, steps, emit, 0)

    def store(t):
        return pltpu.make_async_copy(out.at[t], result.at[t], osem.at[t])

    def settle(t, c):
        copy_o_in(t).wait_recv()
        store(t).start()
        copy_a(t).wait_send()
        copy_b(t).wait_send()
        copy_n(t).wait_send()
        copy_c(t).wait_send()
        copy_d(t).wait_send()
        copy_o(t).wait_send()
        return c

    lax.fori_loop(0, steps, settle, 0)
    for t in range(steps):
        store(t).wait()


VM = pl.BlockSpec(memory_space=pltpu.VMEM)
SM = pl.BlockSpec(memory_space=pltpu.SMEM)
HB = pl.BlockSpec(memory_space=pl.ANY)
DMA = pltpu.SemaphoreType.DMA
LIMIT = 60 << 20


def params(**kw):
    return pltpu.CompilerParams(vmem_limit_bytes=LIMIT, **kw)


def shards(
    tokens, parents, page_request, page_fill, keys_pool, values_pool, decay_pool, gain_attn,
    w_query, w_key, w_value, w_forget, forget_bias, w_out, gain_ffn, w_gate, w_up, w_down,
):
    steps, rows, model = tokens.shape
    heads = w_forget.shape[1]
    width = w_query.shape[0]
    local = rows // BEAMS
    span = steps * BEAMS
    groups = lax.axis_size("group")
    pages = page_request.shape[0]
    ff = w_gate.shape[1]
    sds = jax.ShapeDtypeStruct
    block = (steps, rows, width)
    chain = (pages - SPILL + groups + 1, span, width)
    half = (steps, rows // 2, model)
    return pl.pallas_call(
        functools.partial(group_kernel, groups, local, heads),
        out_shape=sds(tokens.shape, BF16),
        in_specs=[SM, SM, HB, VM, HB, HB, HB, VM, VM, VM, HB, HB, VM, HB, VM, HB, HB, HB],
        out_specs=HB,
        scratch_shapes=[
            pltpu.VMEM(tokens.shape, BF16),
            pltpu.VMEM(block, BF16),
            pltpu.VMEM(tokens.shape, BF16),
            pltpu.VMEM((3, width, model), BF16),
            pltpu.VMEM(keys_pool.shape, BF16),
            pltpu.VMEM(values_pool.shape, BF16),
            pltpu.VMEM((heads, pages, 128), F32),
            pltpu.VMEM(tokens.shape, BF16),
            pltpu.VMEM((local, span, width), BF16),
            pltpu.VMEM(block, BF16),
            pltpu.VMEM(block, BF16),
            pltpu.VMEM(block, BF16),
            pltpu.VMEM(block, F32),
            pltpu.VMEM((8, 128), jnp.int32),
            pltpu.VMEM((groups, 8, 128), jnp.int32),
            pltpu.VMEM((groups, 128), jnp.int32),
            pltpu.VMEM((groups, span, width), BF16),
            pltpu.VMEM((groups, span, width), BF16),
            pltpu.VMEM((groups, span * width // 128 + span // 4, 128), BF16),
            pltpu.VMEM((groups, span * width // 128 + span // 4, 128), BF16),
        ]
        + [pltpu.VMEM(chain, F32)] * 3
        + [pltpu.VMEM(block, F32)] * 4
        + [pltpu.VMEM((SPILL, 128, width), BF16)]
        + [
            pltpu.SMEM((groups, 128), jnp.int32),
            pltpu.SMEM((local,), jnp.int32),
            pltpu.SMEM((groups,), jnp.int32),
            DMA((6,)),
            DMA((1,)),
        ]
        + [DMA((groups,))] * 6
        + [
            pltpu.VMEM((width, model), BF16),
            pltpu.VMEM((model, ff), BF16),
            pltpu.VMEM((model, ff), BF16),
            pltpu.VMEM((ff, model), BF16),
            pltpu.VMEM(half, F32),
            pltpu.VMEM(half, F32),
            pltpu.VMEM((rows, model), F32),
        ]
        + [pltpu.VMEM(half, BF16)] * 8
        + [DMA((4,)), DMA((steps,)), DMA((6, steps)), DMA((6, steps))],
        compiler_params=params(collective_id=0, has_side_effects=True),
        name="layer",
    )(
        page_request, page_fill, tokens, gain_attn, w_query, w_key, w_value, w_forget.T,
        forget_bias[None], parents, keys_pool, values_pool, decay_pool.transpose(1, 0, 2),
        w_out, gain_ffn, w_gate, w_up, w_down,
    )


def solution(mesh):
    return jax.shard_map(
        shards,
        mesh=mesh,
        in_specs=(
            P(None, "group", None),
            P(None, "group"),
            P("group"),
            P("group"),
            P("group", "head", None),
            P("group", "head", None),
            P("group", "head", None),
            P(),
            P("head", None),
            P("head", None),
            P("head", None),
            P(None, "head"),
            P("head"),
            P("head", None),
            P(),
            P(None, "head"),
            P(None, "head"),
            P("head", None),
        ),
        out_specs=P(None, "group", None),
        check_vma=False,
    )
```

```python
import functools

import jax
import jax.numpy as jnp
from jax import lax
from jax.experimental import pallas as pl
from jax.experimental.pallas import tpu as pltpu
from jax.sharding import PartitionSpec as P

BEAMS = 8
OWNED_SLOTS = 32
SPILL = 16
STAT = 128
EPS = 1e-05
MASKED = -1e30
F32 = jnp.float32
BF16 = jnp.bfloat16
MESH = pl.DeviceIdType.MESH


def rms(x, gain):
    return x * lax.rsqrt(jnp.mean(x * x, axis=-1, keepdims=True) + EPS) * gain


def dot(a, b):
    return jnp.dot(a, b, preferred_element_type=F32)


def dot_nt(a, b):
    return lax.dot_general(a, b, (((1,), (1,)), ((), ())), preferred_element_type=F32)


def exact_dot(a, b):
    return jnp.dot(a, b, preferred_element_type=F32, precision=lax.Precision.HIGHEST)


def iota(shape, dim):
    return lax.broadcasted_iota(jnp.int32, shape, dim)


def turn(values):
    return values.astype(F32).T.astype(BF16)


def page_partial(q, masks, keys, values, bias):
    span, width = q.shape
    low = iota((span, 128), 1) < 64
    numer, top, total, tops, totals = [], [], [], [], []
    for j in range(width // 128):
        cut = slice(128 * j, 128 * (j + 1))
        wide = jnp.concatenate([q[:, cut]] * 2, axis=0) * masks
        shift = jnp.concatenate([jnp.broadcast_to(b, (span, 128)) for b in bias[2 * j : 2 * j + 2]], axis=0)
        scores = dot(wide, keys[cut]) + shift
        best = jnp.max(scores, axis=-1, keepdims=True)
        weight = jnp.exp(scores - best)
        whole = jnp.sum(weight, axis=-1, keepdims=True)
        out = dot(weight.astype(BF16), values[:, cut])
        numer.append(jnp.where(low, out[:span], out[span:]))
        best = jnp.broadcast_to(best, (2 * span, 128))
        whole = jnp.broadcast_to(whole, (2 * span, 128))
        top.append(jnp.where(low, best[:span], best[span:]))
        total.append(jnp.where(low, whole[:span], whole[span:]))
        tops += [best[:span], best[span:]]
        totals += [whole[:span], whole[span:]]
    return numer, top, total, tops, totals


def stat_lanes(shape, dim, heads):
    lane = iota(shape, dim)
    place = lane % 32
    return lane // 32, place % heads, place // heads


def pack_stats(tops, totals):
    heads = len(tops)
    quarter = tops[0].shape[0] // 4
    group, head, part = stat_lanes((quarter, STAT), 1, heads)
    value = jnp.zeros((quarter, STAT), F32)
    for g in range(4):
        cut = slice(g * quarter, (g + 1) * quarter)
        for h in range(heads):
            both = jnp.where(part < 3, tops[h][cut], totals[h][cut])
            value = jnp.where((group == g) & (head == h), both, value)
    first = value.astype(BF16).astype(F32)
    rest = value - first
    second = rest.astype(BF16).astype(F32)
    out = jnp.where(part % 3 == 0, first, jnp.where(part % 3 == 1, second, rest - second))
    return jnp.where(part < 5, out, 0.0)


def history(q, k, v, f, parents, numer_out, top_out, total_out, heads):
    steps, rows, width = q.shape
    size = width // heads
    square = (width, width)
    same = jnp.where(iota(square, 0) // size == iota(square, 1) // size, 1.0, 0.0).astype(BF16)
    keys, vals, sums = [], [], []
    for t in range(steps):
        if t > 0:
            lane = iota((rows, rows), 1)
            source = lane - lane % BEAMS + parents[t - 1 : t]
            pick = jnp.where(iota((rows, rows), 0) == source, 1.0, 0.0).T
            pick16 = pick.astype(BF16)
            keys = [dot(pick16, a).astype(BF16) for a in keys]
            vals = [dot(pick16, a).astype(BF16) for a in vals]
            sums = [exact_dot(pick, a) for a in sums]
        keys.append(k[t])
        vals.append(v[t])
        sums.append(f[t] + sums[-1] if t > 0 else f[t])
        asked = q[t].astype(F32)
        scores = []
        for key, total in zip(keys, sums):
            product = asked * key.astype(F32)
            high = product.astype(BF16)
            low = (product - high.astype(F32)).astype(BF16)
            scores.append((dot(high, same) + dot(low, same)) - total)
        best = functools.reduce(jnp.maximum, scores)
        weights = [jnp.exp(s - best) for s in scores]
        top_out[t] = best
        total_out[t] = functools.reduce(jnp.add, weights)
        numer_out[t] = functools.reduce(
            jnp.add, [w.astype(BF16).astype(F32) * a.astype(F32) for w, a in zip(weights, vals)]
        )


def group_kernel(
    groups, local, heads, request, fill, tokens_h, gain_h, wq, wk, wv, wf_h, bias_h, parents_h, keys_h, values_h, decay_h,
    wo_h, gain_ffn_h, wg_h, wu_h, wd_h,
    result,
    out, att_all, tokens, wbuf, keys, values, dec, normed, q_req, q_step, k_new, v_new, f_new,
    table, table_in, loc_v, send, q_in, sent, arrived, s_numer, s_top, s_total, h_numer, h_top, h_total,
    turned,
    loc, last, slot,
    lsem, msem, tsend, trecv, qsend, qrecv, rsend, rrecv,
    wo_all, wg, wu, wd, keep, residual, acc,
    c_tx, c_rx, d_tx, d_rx,
    wsend, wrecv,
    gain, wf, bias, parents, decay, gain_ffn, nsem,
    wsem, osem, sems_s, sems_r,
):
    steps, rows, width = q_step.shape
    span = steps * BEAMS
    pages = keys.shape[0]
    owned = pages - SPILL
    size = width // heads
    blocks = width // 128
    me = lax.axis_index("group")
    half = rows // 2
    head = lax.axis_index("head")
    core = lax.rem(head, 2)
    sibling = {"head": head + 1 - 2 * core}
    far = core + 2 * (1 - head // 2)
    across = {"head": far}
    diagonal = {"head": far + 1 - 2 * core}
    beyond = {"group": me + 1 - 2 * lax.rem(me, 2), "head": far}
    wloads = [
        pltpu.make_async_copy(a, b, wsem.at[i])
        for i, (a, b) in enumerate(((wo_h, wo_all.at[head]), (wg_h, wg), (wu_h, wu), (wd_h, wd)))
    ]
    loads = [
        pltpu.make_async_copy(a, b, lsem.at[i])
        for i, (a, b) in enumerate(
            (
                (tokens_h, tokens),
                (wq, wbuf.at[0]),
                (wk, wbuf.at[1]),
                (wv, wbuf.at[2]),
                (keys_h, keys),
                (values_h, values),
            )
        )
    ]
    for load in loads[:2] + wloads[:1]:
        load.start()
    notes = [
        pltpu.make_async_copy(a, b, nsem.at[i])
        for i, (a, b) in enumerate(
            (
                (gain_h, gain),
                (wf_h, wf),
                (bias_h, bias),
                (parents_h, parents),
                (decay_h, decay),
                (gain_ffn_h, gain_ffn),
            )
        )
    ]
    for note in notes:
        note.start()
    barrier = pltpu.get_barrier_semaphore()

    def peer_of(d):
        return lax.rem(me + d, groups)

    def each_peer(body):
        def step(d, c):
            body(d)
            return c

        lax.fori_loop(1, groups, step, 0)

    each_peer(
        lambda d: pl.semaphore_signal(
            barrier, inc=1, device_id={"group": peer_of(d)}, device_id_type=MESH
        )
    )

    for other in (sibling, across, diagonal, beyond):
        pl.semaphore_signal(barrier, inc=1, device_id=other, device_id_type=MESH)

    def remote(src, dst, ssem, rsem, d):
        return pltpu.make_async_remote_copy(
            src_ref=src,
            dst_ref=dst,
            send_sem=ssem,
            recv_sem=rsem,
            device_id={"group": peer_of(d)},
            device_id_type=MESH,
        )

    def table_copy(d, there):
        return remote(table, table_in.at[there], tsend.at[d], trecv.at[there], d)

    def query_copy(d, there):
        return remote(send.at[peer_of(d)], q_in.at[there], qsend.at[d], qrecv.at[there], d)

    def result_copy(peer, there):
        return pltpu.make_async_remote_copy(
            src_ref=sent.at[peer],
            dst_ref=arrived.at[there],
            send_sem=rsend.at[peer],
            recv_sem=rrecv.at[there],
            device_id={"group": peer},
            device_id_type=MESH,
        )

    lane = iota(table.shape, 1)
    heard = jnp.full(table.shape, -1, jnp.int32)
    for s in range(SPILL):
        heard = jnp.where(lane == s, request[owned + s], heard)
    table[...] = heard
    table_in[pl.ds(me, 1)] = jnp.full((1,) + table.shape, -1, jnp.int32)
    q_in[pl.ds(me, 1)] = jnp.zeros((1, span, width), BF16)
    arrived[pl.ds(me, 1)] = jnp.zeros((1,) + arrived.shape[1:], BF16)
    pl.semaphore_wait(barrier, groups + 3)
    each_peer(lambda d: table_copy(d, me).start())
    part = wo_all.shape[1] // 2
    early = part * 2 // 3

    def weight_copy(kind, ref, device):
        return pltpu.make_async_remote_copy(
            src_ref=ref,
            dst_ref=ref,
            send_sem=wsend.at[kind],
            recv_sem=wrecv.at[kind],
            device_id=device,
            device_id_type=MESH,
        )

    out_weights = [
        weight_copy(0, wo_all.at[head, :early], across),
        weight_copy(1, wo_all.at[head, part : part + early], beyond),
        weight_copy(2, wo_all.at[head], sibling),
        weight_copy(3, wo_all.at[far], sibling),
        weight_copy(4, wo_all.at[head, early:part], across),
        weight_copy(5, wo_all.at[head, part + early :], beyond),
    ]
    in_weights = [
        weight_copy(0, wo_all.at[far, :early], across),
        weight_copy(1, wo_all.at[far, part : part + early], beyond),
        weight_copy(2, wo_all.at[head + 1 - 2 * core], sibling),
        weight_copy(3, wo_all.at[far + 1 - 2 * core], sibling),
        weight_copy(4, wo_all.at[far, early:part], across),
        weight_copy(5, wo_all.at[far, part + early :], beyond),
    ]
    wloads[0].wait()
    for copy in out_weights[:3]:
        copy.start()
    loads[0].wait()
    for note in notes:
        note.wait()

    def norm_step(t, c):
        normed[t] = rms(tokens[t].astype(F32), gain[...]).astype(BF16)
        return c

    lax.fori_loop(0, steps, norm_step, 0)
    for load in loads[2:] + wloads[1:]:
        load.start()
    each_peer(lambda d: table_copy(d, lax.rem(me + d, groups)).wait_recv())
    batch = 8
    for i in range(groups // batch):
        heard = table_in[i * batch : (i + 1) * batch, 0, :]
        where = jnp.max(
            jnp.where(heard // local == me, heard - me * local, -1), axis=-1, keepdims=True
        )
        loc_v[i * batch : (i + 1) * batch] = jnp.broadcast_to(where, (batch, 128))
    to_scalar = pltpu.make_async_copy(loc_v, loc, msem.at[0])
    to_scalar.start()
    loads[1].wait()
    q = dot_nt(normed[...].reshape(steps * rows, normed.shape[-1]), wbuf[0]).astype(BF16).astype(F32) * size ** (-0.5)
    q_req[...] = (
        q.reshape(steps, local, BEAMS, width)
        .transpose(1, 0, 2, 3)
        .reshape(local, span, width)
        .astype(BF16)
    )
    to_scalar.wait()

    def send_query(d):
        peer = peer_of(d)
        send[peer] = q_req[jnp.maximum(loc[peer, 0], 0)]
        query_copy(d, me).start()

    each_peer(send_query)
    q_step[...] = q.astype(BF16).reshape(steps, rows, width)

    loads[2].wait()
    k_new[...] = dot_nt(normed[...].reshape(steps * rows, normed.shape[-1]), wbuf[1]).astype(BF16).reshape(steps, rows, width)
    loads[3].wait()
    v_new[...] = dot_nt(normed[...].reshape(steps * rows, normed.shape[-1]), wbuf[2]).astype(BF16).reshape(steps, rows, width)
    gate = jax.nn.log_sigmoid(dot_nt(normed[...].reshape(steps * rows, normed.shape[-1]), wf[...]) + bias[...])
    spread = jnp.where(iota((heads, width), 1) // size == iota((heads, width), 0), 1.0, 0.0)
    f_new[...] = exact_dot(gate, spread).reshape(steps, rows, width)
    dec[...] = decay[...].astype(F32)
    low = iota((span, 128), 1) < 64
    masks = jnp.concatenate([jnp.where(low, 1.0, 0.0), jnp.where(low, 0.0, 1.0)], axis=0).astype(BF16)

    def bias_of(page):
        inside = iota((1, 128), 1) < fill[page]
        return [jnp.where(inside, dec[h, pl.ds(page, 1), :], MASKED) for h in range(heads)]

    for r in range(local):
        last[r] = 0
    for s in range(groups):
        found = jnp.int32(0)
        for i in range(SPILL):
            found = jnp.where(request[owned + i] // local == s, i, found)
        slot[s] = found
    s_numer[0] = jnp.zeros((span, width), F32)
    s_total[0] = jnp.zeros((span, width), F32)
    s_top[0] = jnp.full((span, width), MASKED, F32)

    def chain(r, entry, numer, top, total):
        before = last[jnp.maximum(r, 0)]
        for j in range(blocks):
            cut = slice(128 * j, 128 * (j + 1))
            old = s_top[before, :, cut]
            best = jnp.maximum(old, top[j])
            keep = jnp.exp(old - best)
            add = jnp.exp(top[j] - best)
            s_numer[entry, :, cut] = s_numer[before, :, cut] * keep + numer[j] * add
            s_total[entry, :, cut] = s_total[before, :, cut] * keep + total[j] * add
            s_top[entry, :, cut] = best
        for i in range(local):
            last[i] = jnp.where(r == i, entry, last[i])

    loads[4].wait()
    loads[5].wait()
    history(q_step, k_new, v_new, f_new, parents, h_numer, h_top, h_total, heads)
    def turn_page(i, c):
        turned[i] = turn(values[owned + i])
        return c

    lax.fori_loop(0, SPILL, turn_page, 0)

    pair = 4

    def hosted(i, c):
        found = []
        for u in range(pair):
            d = i * pair + u
            source = lax.rem(me - d + groups, groups)

            @pl.when(d > 0)
            def _():
                remote(send.at[source], q_in.at[source], qsend.at[0], qrecv.at[source], 1).wait_recv()

        for u in range(pair):
            source = lax.rem(me - (i * pair + u) + groups, groups)
            page = owned + slot[source]
            found.append(
                (source, page_partial(q_in[source], masks, keys.at[page], turned.at[slot[source]], bias_of(page)))
            )
        for source, (numer, _, _, tops, totals) in found:
            for j in range(blocks):
                sent[source, span * j : span * (j + 1)] = numer[j].astype(BF16)
            sent[source, span * blocks :] = pack_stats(tops, totals).astype(BF16)
        for u in range(pair):
            d = i * pair + u
            source = lax.rem(me - d + groups, groups)

            @pl.when(d > 0)
            def _():
                result_copy(source, me).start()

        return c

    lax.fori_loop(0, groups // pair, hosted, 0)
    out_weights[4].start()
    out_weights[5].start()
    unroll = 4

    def own_pages(i, c):
        found = []
        for u in range(unroll):
            page = i * unroll + u
            r = lax.rem(request[page], local)
            found.append(
                (r, page, page_partial(q_req[r], masks, keys.at[page], turn(values[page]), bias_of(page)))
            )
        for r, page, (numer, top, total, _, _) in found:
            chain(r, page + 1, numer, top, total)
        return c

    lax.fori_loop(0, owned // unroll, own_pages, 0)
    for i in (0, 1, 4, 5):
        in_weights[i].wait_recv()
    out_weights[3].start()


    shape = (STAT, 2 * width)
    _, row_head, row_part = stat_lanes(shape, 0, heads)
    col = iota(shape, 1)
    is_total = jnp.where(col >= width, 1, 0)
    expand = (row_part // 3 == is_total) & (row_part < 5) & (row_head == (col - is_total * width) // size)
    expand = jnp.where(expand, 1.0, 0.0).astype(BF16)
    owner, _, _ = stat_lanes((span // 4, STAT), 1, heads)

    four = 4

    def absorb(i, c):
        found = []
        for u in range(four):
            d = i * four + u
            source = peer_of(d)

            @pl.when(d > 0)
            def _():
                result_copy(source, source).wait_recv()

            packed = arrived[source, span * blocks :].astype(F32)
            spread_rows = [jnp.where(owner == g, packed, 0.0) for g in range(4)]
            found.append(jnp.concatenate(spread_rows, axis=0).astype(BF16))
        stats = dot(jnp.concatenate(found, axis=0), expand)
        for u in range(four):
            d = i * four + u
            source = peer_of(d)
            part = stats[span * u : span * (u + 1)]
            cuts = [slice(128 * j, 128 * (j + 1)) for j in range(blocks)]
            numer = [arrived[source, span * j : span * (j + 1)].astype(F32) for j in range(blocks)]
            top = [part[:, cut] for cut in cuts]
            total = [part[:, width + cut.start : width + cut.stop] for cut in cuts]
            chain(loc[source, 0], owned + 1 + d, numer, top, total)
        return c

    lax.fori_loop(0, groups // four, absorb, 0)

    for r in range(local):
        cut = slice(r * BEAMS, (r + 1) * BEAMS)
        entry = last[r]
        shape = (steps, BEAMS, width)
        p_top = s_top[entry].reshape(shape)
        best = jnp.maximum(p_top, h_top[:, cut])
        p_scale = jnp.exp(p_top - best)
        h_scale = jnp.exp(h_top[:, cut] - best)
        whole = s_total[entry].reshape(shape) * p_scale + h_total[:, cut] * h_scale
        mixed = s_numer[entry].reshape(shape) * p_scale + h_numer[:, cut] * h_scale
        h_numer[:, cut] = mixed / whole
    att_all[head] = h_numer[...].astype(BF16)

    def finish(d):
        table_copy(d, me).wait_send()
        query_copy(d, me).wait_send()
        result_copy(peer_of(d), me).wait_send()


    mine = pl.ds(pl.multiple_of(core * half, half), half)
    theirs = pl.ds(pl.multiple_of((1 - core) * half, half), half)
    def pair_copy(kind, t, src, dst, device):
        return pltpu.make_async_remote_copy(
            src_ref=src,
            dst_ref=dst,
            send_sem=sems_s.at[kind, t],
            recv_sem=sems_r.at[kind, t],
            device_id=device,
            device_id_type=MESH,
        )

    copy_a = lambda t: pair_copy(1, t, att_all.at[head, t, mine], att_all.at[head, t, mine], across)
    copy_a_in = lambda t: pair_copy(1, t, att_all.at[far, t, mine], att_all.at[far, t, mine], across)
    near = head + 1 - 2 * core
    cross = far + 1 - 2 * core
    copy_b = lambda t: pair_copy(6, t, att_all.at[head, t, theirs], att_all.at[head, t, theirs], diagonal)
    copy_b_in = lambda t: pair_copy(6, t, att_all.at[cross, t, mine], att_all.at[cross, t, mine], diagonal)
    copy_s = lambda t: pair_copy(0, t, att_all.at[head, t, theirs], att_all.at[head, t, theirs], sibling)
    copy_s_in = lambda t: pair_copy(0, t, att_all.at[near, t, mine], att_all.at[near, t, mine], sibling)
    copy_n = lambda t: pair_copy(2, t, normed.at[t, mine], normed.at[t, mine], sibling)
    copy_n_in = lambda t: pair_copy(2, t, normed.at[t, theirs], normed.at[t, theirs], sibling)
    copy_c = lambda t: pair_copy(3, t, c_tx.at[t], c_rx.at[t], sibling)
    copy_d = lambda t: pair_copy(4, t, d_tx.at[t], d_rx.at[t], across)
    copy_o = lambda t: pair_copy(5, t, out.at[t, mine], out.at[t, mine], sibling)
    copy_o_in = lambda t: pair_copy(5, t, out.at[t, theirs], out.at[t, theirs], sibling)

    def lead(t, c):
        copy_a(t).start()
        copy_b(t).start()
        copy_s(t).start()
        return c

    lax.fori_loop(0, steps, lead, 0)
    in_weights[2].wait_recv()
    in_weights[3].wait_recv()
    for copy in out_weights:
        copy.wait_send()
    each_peer(finish)
    for load in wloads[1:]:
        load.wait()

    def down_cross(t):
        copy_c(t).wait_recv()
        d_tx[t] = (keep[t] + c_rx[t].astype(F32)).astype(BF16)
        copy_d(t).start()

    def feed(t, c):
        copy_a_in(t).wait_recv()
        copy_b_in(t).wait_recv()
        copy_s_in(t).wait_recv()
        res = tokens[t, mine].astype(F32)
        for h in range(wo_all.shape[0]):
            res = res + dot(att_all[h, t, mine], wo_all[h])
        residual[t] = res
        normed[t, mine] = rms(res, gain_ffn[...]).astype(BF16)
        copy_n(t).start()

        @pl.when(t > 0)
        def _():
            down_cross(t - 1)

        copy_n_in(t).wait_recv()
        x = normed[t]
        gate = dot(x, wg[...])
        up = dot(x, wu[...])
        hidden = (gate / (1.0 + jnp.exp(-gate)) * up).astype(BF16)
        acc[...] = dot(hidden, wd[...])
        keep[t] = acc[mine]
        c_tx[t] = acc[theirs].astype(BF16)
        copy_c(t).start()
        return c

    lax.fori_loop(0, steps, feed, 0)
    down_cross(steps - 1)

    def emit(t, c):
        copy_d(t).wait_recv()
        total = residual[t] + (d_tx[t].astype(F32) + d_rx[t].astype(F32))
        out[t, mine] = total.astype(BF16)
        copy_o(t).start()
        return c

    lax.fori_loop(0, steps, emit, 0)

    def store(t):
        return pltpu.make_async_copy(out.at[t], result.at[t], osem.at[t])

    def settle(t, c):
        copy_o_in(t).wait_recv()
        store(t).start()
        copy_a(t).wait_send()
        copy_b(t).wait_send()
        copy_s(t).wait_send()
        copy_n(t).wait_send()
        copy_c(t).wait_send()
        copy_d(t).wait_send()
        copy_o(t).wait_send()
        return c

    lax.fori_loop(0, steps, settle, 0)
    for t in range(steps):
        store(t).wait()


VM = pl.BlockSpec(memory_space=pltpu.VMEM)
SM = pl.BlockSpec(memory_space=pltpu.SMEM)
HB = pl.BlockSpec(memory_space=pl.ANY)
DMA = pltpu.SemaphoreType.DMA
LIMIT = 62 << 20


def params(**kw):
    return pltpu.CompilerParams(vmem_limit_bytes=LIMIT, **kw)


def shards(
    tokens, parents, page_request, page_fill, keys_pool, values_pool, decay_pool, gain_attn,
    w_query, w_key, w_value, w_forget, forget_bias, w_out, gain_ffn, w_gate, w_up, w_down,
):
    steps, rows, model = tokens.shape
    heads = w_forget.shape[1]
    width = w_query.shape[0]
    local = rows // BEAMS
    span = steps * BEAMS
    groups = lax.axis_size("group")
    pages = page_request.shape[0]
    ff = w_gate.shape[1]
    sds = jax.ShapeDtypeStruct
    block = (steps, rows, width)
    chain = (pages - SPILL + groups + 1, span, width)
    half = (steps, rows // 2, model)
    return pl.pallas_call(
        functools.partial(group_kernel, groups, local, heads),
        out_shape=sds(tokens.shape, BF16),
        in_specs=[SM, SM] + [HB] * 16,
        out_specs=HB,
        scratch_shapes=[
            pltpu.VMEM(tokens.shape, BF16),
            pltpu.VMEM((lax.axis_size("head"),) + block, BF16),
            pltpu.VMEM(tokens.shape, BF16),
            pltpu.VMEM((3, width, model), BF16),
            pltpu.VMEM(keys_pool.shape, BF16),
            pltpu.VMEM(values_pool.shape, BF16),
            pltpu.VMEM((heads, pages, 128), F32),
            pltpu.VMEM(tokens.shape, BF16),
            pltpu.VMEM((local, span, width), BF16),
            pltpu.VMEM(block, BF16),
            pltpu.VMEM(block, BF16),
            pltpu.VMEM(block, BF16),
            pltpu.VMEM(block, F32),
            pltpu.VMEM((8, 128), jnp.int32),
            pltpu.VMEM((groups, 8, 128), jnp.int32),
            pltpu.VMEM((groups, 128), jnp.int32),
            pltpu.VMEM((groups, span, width), BF16),
            pltpu.VMEM((groups, span, width), BF16),
            pltpu.VMEM((groups, span * width // 128 + span // 4, 128), BF16),
            pltpu.VMEM((groups, span * width // 128 + span // 4, 128), BF16),
        ]
        + [pltpu.VMEM(chain, F32)] * 3
        + [pltpu.VMEM(block, F32)] * 3
        + [pltpu.VMEM((SPILL, 128, width), BF16)]
        + [
            pltpu.SMEM((groups, 128), jnp.int32),
            pltpu.SMEM((local,), jnp.int32),
            pltpu.SMEM((groups,), jnp.int32),
            DMA((6,)),
            DMA((1,)),
        ]
        + [DMA((groups,))] * 6
        + [
            pltpu.VMEM((lax.axis_size("head"), width, model), BF16),
            pltpu.VMEM((model, ff), BF16),
            pltpu.VMEM((model, ff), BF16),
            pltpu.VMEM((ff, model), BF16),
            pltpu.VMEM(half, F32),
            pltpu.VMEM(half, F32),
            pltpu.VMEM((rows, model), F32),
        ]
        + [pltpu.VMEM(half, BF16)] * 4
        + [DMA((6,)), DMA((6,))]
        + [
            pltpu.VMEM((model,), F32),
            pltpu.VMEM((heads, model), BF16),
            pltpu.VMEM((1, heads), F32),
            pltpu.VMEM(parents.shape, jnp.int32),
            pltpu.VMEM((heads, pages, 128), BF16),
            pltpu.VMEM((model,), F32),
            DMA((6,)),
        ]
        + [DMA((4,)), DMA((steps,)), DMA((7, steps)), DMA((7, steps))],
        compiler_params=params(collective_id=0, has_side_effects=True),
        name="layer",
    )(
        page_request, page_fill, tokens, gain_attn, w_query, w_key, w_value, w_forget.T,
        forget_bias[None], parents, keys_pool, values_pool, decay_pool.transpose(1, 0, 2),
        w_out, gain_ffn, w_gate, w_up, w_down,
    )


def solution(mesh):
    return jax.shard_map(
        shards,
        mesh=mesh,
        in_specs=(
            P(None, "group", None),
            P(None, "group"),
            P("group"),
            P("group"),
            P("group", "head", None),
            P("group", "head", None),
            P("group", "head", None),
            P(),
            P("head", None),
            P("head", None),
            P("head", None),
            P(None, "head"),
            P("head"),
            P("head", None),
            P(),
            P(None, "head"),
            P(None, "head"),
            P("head", None),
        ),
        out_specs=P(None, "group", None),
        check_vma=False,
    )
```

```python
import functools

import jax
import jax.numpy as jnp
from jax import lax
from jax.experimental import pallas as pl
from jax.experimental.pallas import tpu as pltpu
from jax.sharding import PartitionSpec as P

BEAMS = 8
OWNED_SLOTS = 32
SPILL = 16
STAT = 128
EPS = 1e-05
MASKED = -1e30
F32 = jnp.float32
BF16 = jnp.bfloat16
MESH = pl.DeviceIdType.MESH


def rms(x, gain):
    return x * lax.rsqrt(jnp.mean(x * x, axis=-1, keepdims=True) + EPS) * gain


def dot(a, b):
    return jnp.dot(a, b, preferred_element_type=F32)


def dot_nt(a, b):
    return lax.dot_general(a, b, (((1,), (1,)), ((), ())), preferred_element_type=F32)


def exact_dot(a, b):
    return jnp.dot(a, b, preferred_element_type=F32, precision=lax.Precision.HIGHEST)


def iota(shape, dim):
    return lax.broadcasted_iota(jnp.int32, shape, dim)


def turn(values):
    return values.astype(F32).T.astype(BF16)


def page_partial(q, masks, keys, values, bias):
    span, width = q.shape
    low = iota((span, 128), 1) < 64
    numer, top, total, tops, totals = [], [], [], [], []
    for j in range(width // 128):
        cut = slice(128 * j, 128 * (j + 1))
        wide = jnp.concatenate([q[:, cut]] * 2, axis=0) * masks
        shift = jnp.concatenate([jnp.broadcast_to(b, (span, 128)) for b in bias[2 * j : 2 * j + 2]], axis=0)
        scores = dot(wide, keys[cut]) + shift
        best = jnp.max(scores, axis=-1, keepdims=True)
        weight = jnp.exp(scores - best)
        whole = jnp.sum(weight, axis=-1, keepdims=True)
        out = dot(weight.astype(BF16), values[:, cut])
        numer.append(jnp.where(low, out[:span], out[span:]))
        best = jnp.broadcast_to(best, (2 * span, 128))
        whole = jnp.broadcast_to(whole, (2 * span, 128))
        top.append(jnp.where(low, best[:span], best[span:]))
        total.append(jnp.where(low, whole[:span], whole[span:]))
        tops += [best[:span], best[span:]]
        totals += [whole[:span], whole[span:]]
    return numer, top, total, tops, totals


def stat_lanes(shape, dim, heads):
    lane = iota(shape, dim)
    place = lane % 32
    return lane // 32, place % heads, place // heads


def pack_stats(tops, totals):
    heads = len(tops)
    quarter = tops[0].shape[0] // 4
    group, head, part = stat_lanes((quarter, STAT), 1, heads)
    value = jnp.zeros((quarter, STAT), F32)
    for g in range(4):
        cut = slice(g * quarter, (g + 1) * quarter)
        for h in range(heads):
            both = jnp.where(part < 3, tops[h][cut], totals[h][cut])
            value = jnp.where((group == g) & (head == h), both, value)
    first = value.astype(BF16).astype(F32)
    rest = value - first
    second = rest.astype(BF16).astype(F32)
    out = jnp.where(part % 3 == 0, first, jnp.where(part % 3 == 1, second, rest - second))
    return jnp.where(part < 5, out, 0.0)


def history(q, k, v, f, parents, numer_out, top_out, total_out, heads):
    steps, rows, width = q.shape
    size = width // heads
    square = (width, width)
    same = jnp.where(iota(square, 0) // size == iota(square, 1) // size, 1.0, 0.0).astype(BF16)
    keys, vals, sums = [], [], []
    for t in range(steps):
        if t > 0:
            lane = iota((rows, rows), 1)
            source = lane - lane % BEAMS + parents[t - 1 : t]
            pick = jnp.where(iota((rows, rows), 0) == source, 1.0, 0.0).T
            pick16 = pick.astype(BF16)
            keys = [dot(pick16, a).astype(BF16) for a in keys]
            vals = [dot(pick16, a).astype(BF16) for a in vals]
            sums = [exact_dot(pick, a) for a in sums]
        keys.append(k[t])
        vals.append(v[t])
        sums.append(f[t] + sums[-1] if t > 0 else f[t])
        asked = q[t].astype(F32)
        scores = []
        for key, total in zip(keys, sums):
            product = asked * key.astype(F32)
            high = product.astype(BF16)
            low = (product - high.astype(F32)).astype(BF16)
            scores.append((dot(high, same) + dot(low, same)) - total)
        best = functools.reduce(jnp.maximum, scores)
        weights = [jnp.exp(s - best) for s in scores]
        top_out[t] = best
        total_out[t] = functools.reduce(jnp.add, weights)
        numer_out[t] = functools.reduce(
            jnp.add, [w.astype(BF16).astype(F32) * a.astype(F32) for w, a in zip(weights, vals)]
        )


def group_kernel(
    groups, local, heads, request, fill, tokens_h, gain_h, wq, wk, wv, wf_h, bias_h, parents_h, keys_h, values_h, decay_h,
    wo_h, gain_ffn_h, wg_h, wu_h, wd_h,
    result,
    out, att_all, tokens, wbuf, keys, values, dec, normed, q_req, q_step, k_new, v_new, f_new,
    table, table_in, loc_v, send, q_in, sent, arrived, s_numer, s_top, s_total, h_numer, h_top, h_total,
    turned,
    loc, last, slot,
    lsem, msem, tsend, trecv, qsend, qrecv, rsend, rrecv,
    wo_all, wg, wu, wd, keep, residual, acc,
    c_tx, c_rx, d_tx, d_rx,
    wsend, wrecv,
    gain, wf, bias, parents, decay, gain_ffn, nsem,
    wsem, osem, sems_s, sems_r,
):
    steps, rows, width = q_step.shape
    span = steps * BEAMS
    pages = keys.shape[0]
    owned = pages - SPILL
    size = width // heads
    blocks = width // 128
    me = lax.axis_index("group")
    half = rows // 2
    head = lax.axis_index("head")
    core = lax.rem(head, 2)
    sibling = {"head": head + 1 - 2 * core}
    far = core + 2 * (1 - head // 2)
    across = {"head": far}
    diagonal = {"head": far + 1 - 2 * core}
    beyond = {"group": me + 1 - 2 * lax.rem(me, 2), "head": far}
    wloads = [
        pltpu.make_async_copy(a, b, wsem.at[i])
        for i, (a, b) in enumerate(((wo_h, wo_all.at[head]), (wg_h, wg), (wu_h, wu), (wd_h, wd)))
    ]
    loads = [
        pltpu.make_async_copy(a, b, lsem.at[i])
        for i, (a, b) in enumerate(
            (
                (tokens_h, tokens),
                (wq, wbuf.at[0]),
                (wk, wbuf.at[1]),
                (wv, wbuf.at[2]),
                (keys_h, keys),
                (values_h, values),
            )
        )
    ]
    for load in loads[:2] + wloads[:1]:
        load.start()
    notes = [
        pltpu.make_async_copy(a, b, nsem.at[i])
        for i, (a, b) in enumerate(
            (
                (gain_h, gain),
                (wf_h, wf),
                (bias_h, bias),
                (parents_h, parents),
                (decay_h, decay),
                (gain_ffn_h, gain_ffn),
            )
        )
    ]
    for note in notes:
        note.start()
    barrier = pltpu.get_barrier_semaphore()

    def peer_of(d):
        return lax.rem(me + d, groups)

    def each_peer(body):
        def step(d, c):
            body(d)
            return c

        lax.fori_loop(1, groups, step, 0)

    each_peer(
        lambda d: pl.semaphore_signal(
            barrier, inc=1, device_id={"group": peer_of(d)}, device_id_type=MESH
        )
    )

    for other in (sibling, across, diagonal, beyond):
        pl.semaphore_signal(barrier, inc=1, device_id=other, device_id_type=MESH)

    def remote(src, dst, ssem, rsem, d):
        return pltpu.make_async_remote_copy(
            src_ref=src,
            dst_ref=dst,
            send_sem=ssem,
            recv_sem=rsem,
            device_id={"group": peer_of(d)},
            device_id_type=MESH,
        )

    def table_copy(d, there):
        return remote(table, table_in.at[there], tsend.at[d], trecv.at[there], d)

    def query_copy(d, there):
        return remote(send.at[peer_of(d)], q_in.at[there], qsend.at[d], qrecv.at[there], d)

    def result_copy(peer, there):
        return pltpu.make_async_remote_copy(
            src_ref=sent.at[peer],
            dst_ref=arrived.at[there],
            send_sem=rsend.at[peer],
            recv_sem=rrecv.at[there],
            device_id={"group": peer},
            device_id_type=MESH,
        )

    lane = iota(table.shape, 1)
    heard = jnp.full(table.shape, -1, jnp.int32)
    for s in range(SPILL):
        heard = jnp.where(lane == s, request[owned + s], heard)
    table[...] = heard
    table_in[pl.ds(me, 1)] = jnp.full((1,) + table.shape, -1, jnp.int32)
    q_in[pl.ds(me, 1)] = jnp.zeros((1, span, width), BF16)
    arrived[pl.ds(me, 1)] = jnp.zeros((1,) + arrived.shape[1:], BF16)
    pl.semaphore_wait(barrier, groups + 3)
    each_peer(lambda d: table_copy(d, me).start())
    part = wo_all.shape[1] // 2
    early = part * 2 // 3

    def weight_copy(kind, ref, device):
        return pltpu.make_async_remote_copy(
            src_ref=ref,
            dst_ref=ref,
            send_sem=wsend.at[kind],
            recv_sem=wrecv.at[kind],
            device_id=device,
            device_id_type=MESH,
        )

    out_weights = [
        weight_copy(0, wo_all.at[head, :early], across),
        weight_copy(1, wo_all.at[head, part : part + early], beyond),
        weight_copy(2, wo_all.at[head], sibling),
        weight_copy(3, wo_all.at[far], sibling),
        weight_copy(4, wo_all.at[head, early:part], across),
        weight_copy(5, wo_all.at[head, part + early :], beyond),
    ]
    in_weights = [
        weight_copy(0, wo_all.at[far, :early], across),
        weight_copy(1, wo_all.at[far, part : part + early], beyond),
        weight_copy(2, wo_all.at[head + 1 - 2 * core], sibling),
        weight_copy(3, wo_all.at[far + 1 - 2 * core], sibling),
        weight_copy(4, wo_all.at[far, early:part], across),
        weight_copy(5, wo_all.at[far, part + early :], beyond),
    ]
    wloads[0].wait()
    for copy in out_weights[:2]:
        copy.start()
    loads[0].wait()
    for note in notes:
        note.wait()

    def norm_step(t, c):
        normed[t] = rms(tokens[t].astype(F32), gain[...]).astype(BF16)
        return c

    lax.fori_loop(0, steps, norm_step, 0)
    for load in loads[2:] + wloads[1:]:
        load.start()
    each_peer(lambda d: table_copy(d, lax.rem(me + d, groups)).wait_recv())
    batch = 8
    for i in range(groups // batch):
        heard = table_in[i * batch : (i + 1) * batch, 0, :]
        where = jnp.max(
            jnp.where(heard // local == me, heard - me * local, -1), axis=-1, keepdims=True
        )
        loc_v[i * batch : (i + 1) * batch] = jnp.broadcast_to(where, (batch, 128))
    to_scalar = pltpu.make_async_copy(loc_v, loc, msem.at[0])
    to_scalar.start()
    loads[1].wait()
    q = dot_nt(normed[...].reshape(steps * rows, normed.shape[-1]), wbuf[0]).astype(BF16).astype(F32) * size ** (-0.5)
    q_req[...] = (
        q.reshape(steps, local, BEAMS, width)
        .transpose(1, 0, 2, 3)
        .reshape(local, span, width)
        .astype(BF16)
    )
    to_scalar.wait()

    def send_query(d):
        peer = peer_of(d)
        send[peer] = q_req[jnp.maximum(loc[peer, 0], 0)]
        query_copy(d, me).start()

    each_peer(send_query)
    q_step[...] = q.astype(BF16).reshape(steps, rows, width)

    loads[2].wait()
    k_new[...] = dot_nt(normed[...].reshape(steps * rows, normed.shape[-1]), wbuf[1]).astype(BF16).reshape(steps, rows, width)
    loads[3].wait()
    v_new[...] = dot_nt(normed[...].reshape(steps * rows, normed.shape[-1]), wbuf[2]).astype(BF16).reshape(steps, rows, width)
    gate = jax.nn.log_sigmoid(dot_nt(normed[...].reshape(steps * rows, normed.shape[-1]), wf[...]) + bias[...])
    spread = jnp.where(iota((heads, width), 1) // size == iota((heads, width), 0), 1.0, 0.0)
    f_new[...] = exact_dot(gate, spread).reshape(steps, rows, width)
    dec[...] = decay[...].astype(F32)
    low = iota((span, 128), 1) < 64
    masks = jnp.concatenate([jnp.where(low, 1.0, 0.0), jnp.where(low, 0.0, 1.0)], axis=0).astype(BF16)

    def bias_of(page):
        inside = iota((1, 128), 1) < fill[page]
        return [jnp.where(inside, dec[h, pl.ds(page, 1), :], MASKED) for h in range(heads)]

    for r in range(local):
        last[r] = 0
    for s in range(groups):
        found = jnp.int32(0)
        for i in range(SPILL):
            found = jnp.where(request[owned + i] // local == s, i, found)
        slot[s] = found
    s_numer[0] = jnp.zeros((span, width), F32)
    s_total[0] = jnp.zeros((span, width), F32)
    s_top[0] = jnp.full((span, width), MASKED, F32)

    def chain(r, entry, numer, top, total):
        before = last[jnp.maximum(r, 0)]
        for j in range(blocks):
            cut = slice(128 * j, 128 * (j + 1))
            old = s_top[before, :, cut]
            best = jnp.maximum(old, top[j])
            keep = jnp.exp(old - best)
            add = jnp.exp(top[j] - best)
            s_numer[entry, :, cut] = s_numer[before, :, cut] * keep + numer[j] * add
            s_total[entry, :, cut] = s_total[before, :, cut] * keep + total[j] * add
            s_top[entry, :, cut] = best
        for i in range(local):
            last[i] = jnp.where(r == i, entry, last[i])

    loads[4].wait()
    loads[5].wait()
    history(q_step, k_new, v_new, f_new, parents, h_numer, h_top, h_total, heads)
    def turn_page(i, c):
        turned[i] = turn(values[owned + i])
        return c

    lax.fori_loop(0, SPILL, turn_page, 0)

    pair = 4

    def hosted(i, c):
        found = []
        for u in range(pair):
            d = i * pair + u
            source = lax.rem(me - d + groups, groups)

            @pl.when(d > 0)
            def _():
                remote(send.at[source], q_in.at[source], qsend.at[0], qrecv.at[source], 1).wait_recv()

        for u in range(pair):
            source = lax.rem(me - (i * pair + u) + groups, groups)
            page = owned + slot[source]
            found.append(
                (source, page_partial(q_in[source], masks, keys.at[page], turned.at[slot[source]], bias_of(page)))
            )
        for source, (numer, _, _, tops, totals) in found:
            for j in range(blocks):
                sent[source, span * j : span * (j + 1)] = numer[j].astype(BF16)
            sent[source, span * blocks :] = pack_stats(tops, totals).astype(BF16)
        for u in range(pair):
            d = i * pair + u
            source = lax.rem(me - d + groups, groups)

            @pl.when(d > 0)
            def _():
                result_copy(source, me).start()

        return c

    lax.fori_loop(0, groups // pair, hosted, 0)
    out_weights[4].start()
    out_weights[5].start()
    unroll = 4

    def own_pages(i, c):
        found = []
        for u in range(unroll):
            page = i * unroll + u
            r = lax.rem(request[page], local)
            found.append(
                (r, page, page_partial(q_req[r], masks, keys.at[page], turn(values[page]), bias_of(page)))
            )
        for r, page, (numer, top, total, _, _) in found:
            chain(r, page + 1, numer, top, total)
        return c

    lax.fori_loop(0, owned // unroll, own_pages, 0)
    for i in (0, 1, 4, 5):
        in_weights[i].wait_recv()
    out_weights[2].start()
    out_weights[3].start()


    shape = (STAT, 2 * width)
    _, row_head, row_part = stat_lanes(shape, 0, heads)
    col = iota(shape, 1)
    is_total = jnp.where(col >= width, 1, 0)
    expand = (row_part // 3 == is_total) & (row_part < 5) & (row_head == (col - is_total * width) // size)
    expand = jnp.where(expand, 1.0, 0.0).astype(BF16)
    owner, _, _ = stat_lanes((span // 4, STAT), 1, heads)

    four = 4

    def absorb(i, c):
        found = []
        for u in range(four):
            d = i * four + u
            source = peer_of(d)

            @pl.when(d > 0)
            def _():
                result_copy(source, source).wait_recv()

            packed = arrived[source, span * blocks :].astype(F32)
            spread_rows = [jnp.where(owner == g, packed, 0.0) for g in range(4)]
            found.append(jnp.concatenate(spread_rows, axis=0).astype(BF16))
        stats = dot(jnp.concatenate(found, axis=0), expand)
        for u in range(four):
            d = i * four + u
            source = peer_of(d)
            part = stats[span * u : span * (u + 1)]
            cuts = [slice(128 * j, 128 * (j + 1)) for j in range(blocks)]
            numer = [arrived[source, span * j : span * (j + 1)].astype(F32) for j in range(blocks)]
            top = [part[:, cut] for cut in cuts]
            total = [part[:, width + cut.start : width + cut.stop] for cut in cuts]
            chain(loc[source, 0], owned + 1 + d, numer, top, total)
        return c

    lax.fori_loop(0, groups // four, absorb, 0)

    for r in range(local):
        cut = slice(r * BEAMS, (r + 1) * BEAMS)
        entry = last[r]
        shape = (steps, BEAMS, width)
        p_top = s_top[entry].reshape(shape)
        best = jnp.maximum(p_top, h_top[:, cut])
        p_scale = jnp.exp(p_top - best)
        h_scale = jnp.exp(h_top[:, cut] - best)
        whole = s_total[entry].reshape(shape) * p_scale + h_total[:, cut] * h_scale
        mixed = s_numer[entry].reshape(shape) * p_scale + h_numer[:, cut] * h_scale
        h_numer[:, cut] = mixed / whole
    att_all[head] = h_numer[...].astype(BF16)

    def finish(d):
        table_copy(d, me).wait_send()
        query_copy(d, me).wait_send()
        result_copy(peer_of(d), me).wait_send()


    mine = pl.ds(pl.multiple_of(core * half, half), half)
    theirs = pl.ds(pl.multiple_of((1 - core) * half, half), half)
    def pair_copy(kind, t, src, dst, device):
        return pltpu.make_async_remote_copy(
            src_ref=src,
            dst_ref=dst,
            send_sem=sems_s.at[kind, t],
            recv_sem=sems_r.at[kind, t],
            device_id=device,
            device_id_type=MESH,
        )

    copy_a = lambda t: pair_copy(1, t, att_all.at[head, t, mine], att_all.at[head, t, mine], across)
    copy_a_in = lambda t: pair_copy(1, t, att_all.at[far, t, mine], att_all.at[far, t, mine], across)
    near = head + 1 - 2 * core
    cross = far + 1 - 2 * core
    copy_b = lambda t: pair_copy(6, t, att_all.at[head, t, theirs], att_all.at[head, t, theirs], diagonal)
    copy_b_in = lambda t: pair_copy(6, t, att_all.at[cross, t, mine], att_all.at[cross, t, mine], diagonal)
    copy_s = lambda t: pair_copy(0, t, att_all.at[head, t, theirs], att_all.at[head, t, theirs], sibling)
    copy_s_in = lambda t: pair_copy(0, t, att_all.at[near, t, mine], att_all.at[near, t, mine], sibling)
    copy_n = lambda t: pair_copy(2, t, normed.at[t, mine], normed.at[t, mine], sibling)
    copy_n_in = lambda t: pair_copy(2, t, normed.at[t, theirs], normed.at[t, theirs], sibling)
    copy_c = lambda t: pair_copy(3, t, c_tx.at[t], c_rx.at[t], sibling)
    copy_d = lambda t: pair_copy(4, t, d_tx.at[t], d_rx.at[t], across)
    copy_o = lambda t: pair_copy(5, t, out.at[t, mine], out.at[t, mine], sibling)
    copy_o_in = lambda t: pair_copy(5, t, out.at[t, theirs], out.at[t, theirs], sibling)

    def lead(t, c):
        copy_a(t).start()
        copy_b(t).start()
        copy_s(t).start()
        return c

    lax.fori_loop(0, steps, lead, 0)
    in_weights[2].wait_recv()
    in_weights[3].wait_recv()
    for copy in out_weights:
        copy.wait_send()
    each_peer(finish)
    for load in wloads[1:]:
        load.wait()

    def down_cross(t):
        copy_c(t).wait_recv()
        d_tx[t] = (keep[t] + c_rx[t].astype(F32)).astype(BF16)
        copy_d(t).start()

    def mix(t):
        copy_a_in(t).wait_recv()
        copy_b_in(t).wait_recv()
        copy_s_in(t).wait_recv()
        res = tokens[t, mine].astype(F32)
        for h in range(wo_all.shape[0]):
            res = res + dot(att_all[h, t, mine], wo_all[h])
        residual[t] = res
        normed[t, mine] = rms(res, gain_ffn[...]).astype(BF16)
        copy_n(t).start()

    def feed(t, c):
        copy_n_in(t).wait_recv()
        x = normed[t]
        gate = dot(x, wg[...])
        up = dot(x, wu[...])
        hidden = (gate / (1.0 + jnp.exp(-gate)) * up).astype(BF16)
        acc[...] = dot(hidden, wd[...])
        keep[t] = acc[mine]
        c_tx[t] = acc[theirs].astype(BF16)
        copy_c(t).start()

        @pl.when(t + 1 < steps)
        def _():
            mix(t + 1)

        down_cross(t)
        return c

    mix(0)
    lax.fori_loop(0, steps, feed, 0)

    def emit(t, c):
        copy_d(t).wait_recv()
        total = residual[t] + (d_tx[t].astype(F32) + d_rx[t].astype(F32))
        out[t, mine] = total.astype(BF16)
        copy_o(t).start()
        return c

    lax.fori_loop(0, steps, emit, 0)

    def store(t):
        return pltpu.make_async_copy(out.at[t], result.at[t], osem.at[t])

    def settle(t, c):
        copy_o_in(t).wait_recv()
        store(t).start()
        copy_a(t).wait_send()
        copy_b(t).wait_send()
        copy_s(t).wait_send()
        copy_n(t).wait_send()
        copy_c(t).wait_send()
        copy_d(t).wait_send()
        copy_o(t).wait_send()
        return c

    lax.fori_loop(0, steps, settle, 0)
    for t in range(steps):
        store(t).wait()


VM = pl.BlockSpec(memory_space=pltpu.VMEM)
SM = pl.BlockSpec(memory_space=pltpu.SMEM)
HB = pl.BlockSpec(memory_space=pl.ANY)
DMA = pltpu.SemaphoreType.DMA
LIMIT = 62 << 20


def params(**kw):
    return pltpu.CompilerParams(vmem_limit_bytes=LIMIT, **kw)


def shards(
    tokens, parents, page_request, page_fill, keys_pool, values_pool, decay_pool, gain_attn,
    w_query, w_key, w_value, w_forget, forget_bias, w_out, gain_ffn, w_gate, w_up, w_down,
):
    steps, rows, model = tokens.shape
    heads = w_forget.shape[1]
    width = w_query.shape[0]
    local = rows // BEAMS
    span = steps * BEAMS
    groups = lax.axis_size("group")
    pages = page_request.shape[0]
    ff = w_gate.shape[1]
    sds = jax.ShapeDtypeStruct
    block = (steps, rows, width)
    chain = (pages - SPILL + groups + 1, span, width)
    half = (steps, rows // 2, model)
    return pl.pallas_call(
        functools.partial(group_kernel, groups, local, heads),
        out_shape=sds(tokens.shape, BF16),
        in_specs=[SM, SM] + [HB] * 16,
        out_specs=HB,
        scratch_shapes=[
            pltpu.VMEM(tokens.shape, BF16),
            pltpu.VMEM((lax.axis_size("head"),) + block, BF16),
            pltpu.VMEM(tokens.shape, BF16),
            pltpu.VMEM((3, width, model), BF16),
            pltpu.VMEM(keys_pool.shape, BF16),
            pltpu.VMEM(values_pool.shape, BF16),
            pltpu.VMEM((heads, pages, 128), F32),
            pltpu.VMEM(tokens.shape, BF16),
            pltpu.VMEM((local, span, width), BF16),
            pltpu.VMEM(block, BF16),
            pltpu.VMEM(block, BF16),
            pltpu.VMEM(block, BF16),
            pltpu.VMEM(block, F32),
            pltpu.VMEM((8, 128), jnp.int32),
            pltpu.VMEM((groups, 8, 128), jnp.int32),
            pltpu.VMEM((groups, 128), jnp.int32),
            pltpu.VMEM((groups, span, width), BF16),
            pltpu.VMEM((groups, span, width), BF16),
            pltpu.VMEM((groups, span * width // 128 + span // 4, 128), BF16),
            pltpu.VMEM((groups, span * width // 128 + span // 4, 128), BF16),
        ]
        + [pltpu.VMEM(chain, F32)] * 3
        + [pltpu.VMEM(block, F32)] * 3
        + [pltpu.VMEM((SPILL, 128, width), BF16)]
        + [
            pltpu.SMEM((groups, 128), jnp.int32),
            pltpu.SMEM((local,), jnp.int32),
            pltpu.SMEM((groups,), jnp.int32),
            DMA((6,)),
            DMA((1,)),
        ]
        + [DMA((groups,))] * 6
        + [
            pltpu.VMEM((lax.axis_size("head"), width, model), BF16),
            pltpu.VMEM((model, ff), BF16),
            pltpu.VMEM((model, ff), BF16),
            pltpu.VMEM((ff, model), BF16),
            pltpu.VMEM(half, F32),
            pltpu.VMEM(half, F32),
            pltpu.VMEM((rows, model), F32),
        ]
        + [pltpu.VMEM(half, BF16)] * 4
        + [DMA((6,)), DMA((6,))]
        + [
            pltpu.VMEM((model,), F32),
            pltpu.VMEM((heads, model), BF16),
            pltpu.VMEM((1, heads), F32),
            pltpu.VMEM(parents.shape, jnp.int32),
            pltpu.VMEM((heads, pages, 128), BF16),
            pltpu.VMEM((model,), F32),
            DMA((6,)),
        ]
        + [DMA((4,)), DMA((steps,)), DMA((7, steps)), DMA((7, steps))],
        compiler_params=params(collective_id=0, has_side_effects=True),
        name="layer",
    )(
        page_request, page_fill, tokens, gain_attn, w_query, w_key, w_value, w_forget.T,
        forget_bias[None], parents, keys_pool, values_pool, decay_pool.transpose(1, 0, 2),
        w_out, gain_ffn, w_gate, w_up, w_down,
    )


def solution(mesh):
    return jax.shard_map(
        shards,
        mesh=mesh,
        in_specs=(
            P(None, "group", None),
            P(None, "group"),
            P("group"),
            P("group"),
            P("group", "head", None),
            P("group", "head", None),
            P("group", "head", None),
            P(),
            P("head", None),
            P("head", None),
            P("head", None),
            P(None, "head"),
            P("head"),
            P("head", None),
            P(),
            P(None, "head"),
            P(None, "head"),
            P("head", None),
        ),
        out_specs=P(None, "group", None),
        check_vma=False,
    )
```
